512 devices in a mesh: seq: 64 (over y, z), head: 8 (over x, core).
Axes of the slice: x: 4, y: 4, z: 16, core: 2. Of those that a mesh axis runs over, the one named last changes fastest.
Arguments:
- lengths: int32 [2], replicated, may hold values from 1 to 3571, 5952 in all
- step_index: int32 [2], replicated, may hold values from 20 to 999
- query_act: bfloat16 [6144, 3072], P('seq', 'head'), may hold values from -24 to 24
- key_act: bfloat16 [6144, 3072], P('seq', 'head'), may hold values from -24 to 24
- value_act: bfloat16 [6144, 3072], P('seq', 'head'), may hold values from -6 to 6
- hidden: bfloat16 [6144, 3072], P('seq', 'head'), may hold values from -64 to 64
- attn_weight: bfloat16 [3072, 3072], P('head'), may hold values from -0.4375 to 0.4375
- gate_mod: bfloat16 [2, 3072], P(None, 'head'), may hold values from 0.5 to 2
- shift_mod: bfloat16 [2, 3072], P(None, 'head'), may hold values from -3 to 3
- scale_mod: bfloat16 [2, 3072], P(None, 'head'), may hold values from -0.5 to 0.5
- proj_weight: bfloat16 [3072, 64], P('head'), may hold values from -0.109375 to 0.109375
- latent: float32 [6144, 64], P('seq'), may hold values from -6 to 6
Outputs:
- hidden_out: bfloat16 [6144, 3072], P('seq', 'head')
- clean_estimate: float32 [6144, 64], P('seq')
- latent_prev: float32 [6144, 64], P('seq')
- latent_rim: float32 [5760, 64], P('seq')
The draws below stay inside these ranges and needn't reach their ends.
Inputs may be any that keep to these rules, and one draw needn't show every extreme that they name: lengths[0] and lengths[1] are laid end to end from slot 0; they sum to 5952 and the larger is at most 3571.
All inputs are finite; a program needn't handle non-finite values.
Results may differ from the reference program's by a relative error of at most 0.008.
Values may be sent and summed in bfloat16 or wider, within the bound.
No kernel may reach another device: no remote copies, remote signals or barrier semaphores. Data moves between devices by JAX's collectives and lax.ppermute only.
A program may use at most 64 MiB of HBM per device.

```python
import math
import jax
import jax.numpy as jnp
import numpy as np
from jax import lax

D = 3072
HEADS = 48
HD = 64
PATCH_CH = 64
TOK_DEV = 96
RIM = 45
TRAIN_STEPS = 1000
STEP_GAP = 20
TOKENS = 6144
LEN_ALL = 5952
LEN_MOST = 3571
N_SEQ = 64


def attention_pair(key):
    base = jax.random.fold_in(key, 101)
    first_key, second_key = jax.random.split(base, 2)
    shape = (TOKENS, HEADS * HD)
    query_vals = 1.5 * jnp.clip(jax.random.normal(first_key, shape, jnp.float32), -4.0, 4.0)
    key_vals = 1.5 * jnp.clip(jax.random.normal(second_key, shape, jnp.float32), -4.0, 4.0)
    return (query_vals, key_vals)


def draw_query_act(key, part):
    return attention_pair(key)[0].astype(jnp.bfloat16)


def draw_key_act(key, part):
    return attention_pair(key)[1].astype(jnp.bfloat16)


def draw_hidden(key, part):
    noise_key, column_key = jax.random.split(jax.random.fold_in(key, 202), 2)
    columns = jnp.arange(D, dtype=jnp.float32)
    column_scale = (1.0 + 2.0 * columns / D) * jnp.exp(jax.random.uniform(column_key, (D,), jnp.float32, 0.0, math.log(3.0)))
    values_out = jnp.clip(jax.random.normal(noise_key, (TOKENS, D), jnp.float32), -4.0, 4.0) * column_scale[None, :]
    return values_out.astype(jnp.bfloat16)


def levels(own_key, shape, shards, smallest, high):
    def one(dim, blocks):
        steps = jax.random.uniform(jax.random.fold_in(jax.random.fold_in(own_key, 6), dim), (blocks,), jnp.float32, smallest / len(shards), high / len(shards))
        return jnp.repeat(jnp.exp(steps), shape[dim] // blocks).reshape((-1,) + (1,) * (len(shape) - dim - 1))

    loudness = one(*shards[0])
    for cut in shards[1:]:
        loudness = loudness * one(*cut)
    return loudness


def length_profile(amount, total, reach, skew):
    weights = [(1 << 20) // math.isqrt(grade ** skew) + 1 for grade in range(2, amount + 1)]
    spare, holding = total - reach - (amount - 1), [1] * (amount - 1)
    while spare > 0:
        movable = [i for i in range(amount - 1) if holding[i] < reach]
        whole, budget = sum([weights[i] for i in movable]), spare
        for i in movable:
            extra = min(reach - holding[i], max(1, budget * weights[i] // whole), spare)
            holding[i] = holding[i] + extra
            spare = spare - extra
    return np.array([reach] + holding)


def uneven(own_key, number_of, total, most, lean):
    if number_of == 2:
        one = jax.random.randint(own_key, (), max(1, total - most), min(most, total - 1) + 1)
        return jnp.stack([one, total - one])
    sizes = jnp.asarray(length_profile(number_of, total, most, lean), jnp.int32)
    pairs = (number_of - 1) // 2
    donor, sink = sizes[1:1 + 2 * pairs:2], sizes[2:2 + 2 * pairs:2]
    margin = jnp.minimum(donor - 1, most - sink)
    moved = jax.random.randint(jax.random.fold_in(own_key, 1), (pairs,), 0, 1 << 20) % (margin + 1)
    sizes = sizes.at[1:1 + 2 * pairs:2].set(donor - moved).at[2:2 + 2 * pairs:2].set(sink + moved)
    return sizes[jax.random.permutation(jax.random.fold_in(own_key, 2), number_of)]


def centred(stream_key, dims, spread, bound, cuts=(), kind=jnp.bfloat16):
    entries = spread * jax.random.normal(stream_key, dims, jnp.float32)
    if cuts:
        entries = entries * levels(stream_key, dims, cuts, -0.22, 0.18)
    return jnp.clip(entries, -bound, bound).astype(kind)


def setup_inputs(seed: int = 0) -> dict:
    keys = jax.random.split(jax.random.key(seed), 13)
    return {
        "lengths": uneven(keys[0], 2, LEN_ALL, LEN_MOST, 0).astype(jnp.int32),
        "step_index": jax.random.randint(keys[1], (2,), STEP_GAP, TRAIN_STEPS).astype(jnp.int32),
        "query_act": draw_query_act(jax.random.fold_in(keys[12], 71), 0),
        "key_act": draw_key_act(jax.random.fold_in(keys[12], 71), 0),
        "value_act": centred(keys[4], (TOKENS, HEADS * HD), 1.0, 6.0, ((0, 64), (1, 8))),
        "hidden": draw_hidden(jax.random.fold_in(keys[12], 71), 0),
        "attn_weight": centred(keys[6], (HEADS * HD, D), (HEADS * HD // 16) ** -0.5, 0.4375, ((0, 8),)),
        "gate_mod": jnp.clip(0.5 + 1.5 * jax.random.uniform(keys[7], (2, D), jnp.float32) ** levels(keys[7], (2, D), ((1, 8),), -0.2, 0.2), 0.5, 2.0).astype(jnp.bfloat16),
        "shift_mod": centred(keys[8], (2, D), 0.5, 3.0, ((1, 8),)),
        "scale_mod": jnp.clip(jax.random.uniform(keys[9], (2, D), jnp.float32, -0.5, 0.5) * levels(keys[9], (2, D), ((1, 8),), -0.4, 0.0), -0.5, 0.5).astype(jnp.bfloat16),
        "proj_weight": centred(keys[10], (D, PATCH_CH), D ** -0.5, 0.109375, ((0, 8),)),
        "latent": centred(keys[11], (TOKENS, PATCH_CH), 1.0, 6.0, ((0, 64),), jnp.float32),
    }


NEG_BIG = -1e+30
EPSILON = 1e-06

def alpha_table():
    betas = jnp.linspace(0.00085 ** 0.5, 0.012 ** 0.5, TRAIN_STEPS, dtype=jnp.float32) ** 2
    return jnp.cumprod(1.0 - betas)

def request_of(position, lengths):
    first_len = lengths[0]
    total_len = lengths[0] + lengths[1]
    return jnp.where(position < 0, -1, jnp.where(position < first_len, 0, jnp.where(position < total_len, 1, 2))).astype(jnp.int32)

def head_attention(query_h, key_h, value_h, requests):
    block_rows = TOK_DEV * 8

    def one_block(number):
        query_b = lax.dynamic_slice_in_dim(query_h, number * block_rows, block_rows, 0)
        req_b = lax.dynamic_slice_in_dim(requests, number * block_rows, block_rows, 0)
        scores = jnp.dot(query_b, key_h.T, preferred_element_type=jnp.float32) / math.sqrt(HD)
        allowed = (req_b[:, None] == requests[None, :]) & (req_b[:, None] < 2)
        scores = jnp.where(allowed, scores, NEG_BIG)
        row_max = lax.optimization_barrier(jnp.max(scores, axis=1))
        weights = jnp.where(allowed, jnp.exp(scores - row_max[:, None]), 0.0)
        row_sum = lax.optimization_barrier(jnp.sum(weights, axis=1))
        mixed = jnp.dot(weights.astype(jnp.bfloat16), value_h, preferred_element_type=jnp.float32)
        return mixed / jnp.where(req_b < 2, row_sum, 1.0)[:, None]
    blocks = lax.map(one_block, jnp.arange(TOKENS // block_rows, dtype=jnp.int32))
    return blocks.reshape(TOKENS, HD)

def column_slice(array, index):
    return lax.dynamic_slice_in_dim(array, index * HD, HD, 1)

def per_row(table, requests):
    first_row = table[0].astype(jnp.float32)
    second_row = table[1].astype(jnp.float32)
    return jnp.where((requests == 0)[:, None], first_row[None], jnp.where((requests == 1)[:, None], second_row[None], 0.0))

def reference(lengths, step_index, query_act, key_act, value_act, hidden, attn_weight, gate_mod, shift_mod, scale_mod, proj_weight, latent):
    requests = request_of(jnp.arange(TOKENS, dtype=jnp.int32), lengths)

    def per_head(index):
        return head_attention(column_slice(query_act, index), column_slice(key_act, index), column_slice(value_act, index), requests)
    heads_out = lax.map(per_head, jnp.arange(HEADS, dtype=jnp.int32))
    attended = jnp.transpose(heads_out, (1, 0, 2)).reshape(TOKENS, HEADS * HD).astype(jnp.bfloat16)
    projected = jnp.dot(attended, attn_weight, preferred_element_type=jnp.float32)
    hidden_out = (hidden.astype(jnp.float32) + per_row(gate_mod, requests) * projected).astype(jnp.bfloat16)
    values_f = hidden_out.astype(jnp.float32)
    row_mean = lax.optimization_barrier(jnp.sum(values_f, axis=1)) / D
    variance = lax.optimization_barrier(jnp.sum(values_f * values_f, axis=1)) / D - row_mean * row_mean
    normed = (values_f - row_mean[:, None]) * lax.rsqrt(variance[:, None] + EPSILON)
    modulated = (normed * (1.0 + per_row(scale_mod, requests)) + per_row(shift_mod, requests)).astype(jnp.bfloat16)
    velocity = jnp.dot(modulated, proj_weight, preferred_element_type=jnp.float32)
    table = alpha_table()
    alpha_now = table[step_index]
    alpha_prev = table[step_index - STEP_GAP]
    now_rows = jnp.where(requests == 0, alpha_now[0], alpha_now[1])[:, None]
    prev_rows = jnp.where(requests == 0, alpha_prev[0], alpha_prev[1])[:, None]
    clean = jnp.sqrt(now_rows) * latent - jnp.sqrt(1.0 - now_rows) * velocity
    noise = jnp.sqrt(1.0 - now_rows) * latent + jnp.sqrt(now_rows) * velocity
    stepped = jnp.sqrt(prev_rows) * clean + jnp.sqrt(1.0 - prev_rows) * noise
    live = (requests < 2)[:, None]
    clean = jnp.where(live, clean, 0.0)
    stepped = jnp.where(live, stepped, 0.0)
    padded = jnp.pad(stepped, ((RIM, RIM), (0, 0)))
    req_pad = jnp.pad(requests, (RIM, RIM), constant_values=-1)
    device_ids = jnp.arange(N_SEQ, dtype=jnp.int32)
    offsets = jnp.arange(RIM, dtype=jnp.int32)
    lower_idx = device_ids[:, None] * TOK_DEV + offsets[None, :]
    upper_idx = (device_ids[:, None] + 1) * TOK_DEV + RIM + offsets[None, :]
    lower_ok = req_pad[lower_idx] == requests[device_ids * TOK_DEV][:, None]
    upper_ok = req_pad[upper_idx] == requests[(device_ids + 1) * TOK_DEV - 1][:, None]
    lower_rows = jnp.where(lower_ok[:, :, None], padded[lower_idx], 0.0)
    upper_rows = jnp.where(upper_ok[:, :, None], padded[upper_idx], 0.0)
    rims = jnp.concatenate([lower_rows, upper_rows], axis=1).reshape(N_SEQ * 2 * RIM, PATCH_CH)
    return (hidden_out, clean, stepped, rims)
```

```python
import jax
import jax.numpy as jnp
import numpy as np
from jax import lax
from jax.experimental import pallas as pl
from jax.experimental.pallas import tpu as pltpu
from jax.sharding import Mesh
from jax.sharding import PartitionSpec as P

D = 3072
HD = 64
RIM = 45
TOK = 96
HALF = 48
LEN_ALL = 5952
TRAIN_STEPS = 1000
STEP_GAP = 20
NY, NZ, NX, NC = 4, 16, 4, 2
NHEAD = 8
EPSILON = 1e-06
MASKED = -1e30
FLOOR = -0.5e30
HEAD_OF = (0, 0, 0, 1, 1, 1, 2, 2, 2, 3, 3, 3, 4, 4, 5, 5)
PART_OF = (0, 1, 2, 0, 1, 2, 0, 1, 2, 0, 1, 2, 0, 1, 0, 1)
SIZE_OF = (32,) * 12 + (48,) * 4
BF = jnp.bfloat16
F32 = jnp.float32
SMEM = pltpu.SMEM
VMEM = pltpu.VMEM


def low_lanes(rows):
    return lax.broadcasted_iota(jnp.int32, (rows, 128), 1) < HD


def swap(x):
    return pltpu.roll(x, HD, 1)


def pack_kernel(q_ref, k_ref, v_ref, out_ref):
    low_h, low_t = low_lanes(HALF), low_lanes(TOK)
    for pair in range(3):
        lanes = slice(128 * pair, 128 * pair + 128)
        q = q_ref[:, lanes].astype(F32) * 0.125
        k = k_ref[:, lanes].astype(F32)
        v = v_ref[:, lanes].astype(F32)
        top, bottom = q[:HALF], q[HALF:]
        queries = (jnp.where(low_h, top, swap(bottom)), jnp.where(low_h, swap(top), bottom))
        keyvals = (jnp.where(low_t, k, swap(v)), jnp.where(low_t, swap(k), v))
        for side in range(2):
            qh = queries[side].astype(BF)
            kvh = keyvals[side].astype(BF)
            for d in range(NZ):
                if HEAD_OF[d] != 2 * pair + side:
                    continue
                size = SIZE_OF[d]
                start = PART_OF[d] * size
                out_ref[d, :HALF, :] = qh
                out_ref[d, HALF : HALF + size, :] = kvh[start : start + size]
                if size < HALF:
                    out_ref[d, HALF + size :, :] = jnp.zeros((HALF - size, 128), BF)


def pieces(x):
    hi = x.astype(BF).astype(F32)
    rest = x - hi
    mid = rest.astype(BF).astype(F32)
    return (hi, mid, rest - mid)


QT = 192
KT = 768


def attend_kernel(scal_ref, q_ref, kv_ref, out_ref, klo_ref, khi_ref, vlo_ref, vhi_ref):
    first_len, row, size, offset = scal_ref[0], scal_ref[1], scal_ref[2], scal_ref[3]
    low = low_lanes(KT)
    lane = lax.broadcasted_iota(jnp.int32, (KT, 128), 1)
    for j in range(NY):
        kv = kv_ref[j * KT : (j + 1) * KT, :].astype(F32)
        other = swap(kv)
        shape = (NZ, HALF, 128)
        slot = lax.broadcasted_iota(jnp.int32, shape, 1)
        pos = (lax.broadcasted_iota(jnp.int32, shape, 0) + j * NZ) * TOK + slot + offset
        pos = jnp.where(slot < size, pos, LEN_ALL).reshape(KT, 128)
        own = jnp.where(pos < first_len, 0, jnp.where(pos < LEN_ALL, 1, -1))
        lo_mask = jnp.where((lane < 3) & (lane != own), MASKED, 0.0).astype(BF)
        hi_mask = jnp.where((lane >= 3) & (lane < 6) & (lane - 3 != own), MASKED, 0.0).astype(BF)
        rows = slice(j * KT, (j + 1) * KT)
        klo_ref[rows, :128] = jnp.where(low, kv, 0.0).astype(BF)
        khi_ref[rows, :128] = jnp.where(low, 0.0, other).astype(BF)
        klo_ref[rows, 128:] = lo_mask
        khi_ref[rows, 128:] = hi_mask
        vlo_ref[rows, :] = jnp.where(low, other, 0.0).astype(BF)
        vhi_ref[rows, :] = jnp.where(low, 0.0, kv).astype(BF)

    low_q = low_lanes(QT)
    lane_q = lax.broadcasted_iota(jnp.int32, (QT, 128), 1)
    blocks = QT // HALF
    eye = (
        lax.broadcasted_iota(jnp.int32, (HALF, 128), 0)
        == lax.broadcasted_iota(jnp.int32, (HALF, 128), 1)
    ).astype(BF)

    def tile(t, carry):
        q = q_ref[pl.ds(t * blocks, blocks), :HALF, :].reshape(QT, 128)
        shape = (blocks, HALF, 128)
        base = (lax.broadcasted_iota(jnp.int32, shape, 0) + row * NZ + t * blocks) * TOK
        pos = (base + lax.broadcasted_iota(jnp.int32, shape, 1)).reshape(QT, 128)
        pos = jnp.where(lane_q < 3, pos, pos + HALF)
        own = jnp.where(pos < first_len, 0, jnp.where(pos < LEN_ALL, 1, 2))
        own = jnp.where(lane_q < 3, own, own + 3)
        q_all = jnp.concatenate([q, jnp.where(lane_q == own, 1.0, 0.0).astype(BF)], axis=1)

        def scores(keys):
            return lax.dot_general(
                q_all, keys, (((1,), (1,)), ((), ())), preferred_element_type=F32
            )

        def soft(k_ref):
            s = scores(k_ref[...])
            m = jnp.maximum(jnp.max(s, axis=1, keepdims=True), FLOOR)
            p = jnp.exp(s - m)
            return m, jnp.sum(p, axis=1, keepdims=True), p.astype(BF)

        m_lo, l_lo, p_lo = soft(klo_ref)
        acc = jnp.dot(p_lo, vlo_ref[...], preferred_element_type=F32)
        m_hi, l_hi, p_hi = soft(khi_ref)
        acc += jnp.dot(p_hi, vhi_ref[...], preferred_element_type=F32)
        div_lo = jnp.where(l_lo > 0.0, l_lo, 1.0)
        div_hi = jnp.where(l_hi > 0.0, l_hi, 1.0)
        out = (acc / jnp.where(low_q, div_lo, div_hi)).astype(BF)
        stats = jnp.zeros((QT, 128), F32)
        number = 0
        for value in (m_lo, l_lo, m_hi, l_hi):
            for piece in pieces(value):
                stats = jnp.where(lane_q == number, piece, stats)
                number += 1
        stats = stats.astype(BF)
        for b in range(blocks):
            rows = slice(b * HALF, (b + 1) * HALF)
            out_ref[t * blocks + b, :HALF, :] = out[rows]
            turned = lax.dot_general(
                stats[rows], eye, (((0,), (0,)), ((), ())), preferred_element_type=F32
            )
            out_ref[t * blocks + b, HALF:, :] = turned[:16].astype(BF)
        return carry

    lax.fori_loop(0, NZ * HALF // QT, tile, 0)


def merge_kernel(part_ref, w_ref, out_ref, att_ref):
    @pl.when(pl.program_id(0) == 0)
    def _():
        low = low_lanes(HALF)
        rows16 = lax.broadcasted_iota(jnp.int32, (16, 128), 0)
        lanes16 = lax.broadcasted_iota(jnp.int32, (16, 128), 1)
        eye = (rows16 == lanes16).astype(BF)
        stats = []
        for d in range(NZ):
            turned = lax.dot_general(
                part_ref[d, HALF:, :], eye, (((0,), (0,)), ((), ())), preferred_element_type=F32
            )[:HALF]
            cols = [turned[:, i : i + 1] for i in range(12)]
            stats.append([cols[3 * i] + cols[3 * i + 1] + cols[3 * i + 2] for i in range(4)])
        heads = []
        for h in range(6):
            devices = [d for d in range(NZ) if HEAD_OF[d] == h]
            shares = []
            for side in range(2):
                tops = [stats[d][2 * side] for d in devices]
                sums = [stats[d][2 * side + 1] for d in devices]
                top = tops[0]
                for m in tops[1:]:
                    top = jnp.maximum(top, m)
                scaled = [jnp.exp(m - top) * s for m, s in zip(tops, sums)]
                total = scaled[0]
                for s in scaled[1:]:
                    total = total + s
                total = jnp.where(total > 0.0, total, 1.0)
                shares.append([s / total for s in scaled])
            mixed = jnp.zeros((HALF, 128), F32)
            for i, d in enumerate(devices):
                weight = jnp.where(low, shares[0][i], shares[1][i])
                mixed += weight * part_ref[d, :HALF, :].astype(F32)
            heads.append(mixed)
        for pair in range(3):
            even, odd = heads[2 * pair], heads[2 * pair + 1]
            lanes = slice(128 * pair, 128 * pair + 128)
            att_ref[:HALF, lanes] = jnp.where(low, even, swap(odd)).astype(BF)
            att_ref[HALF:, lanes] = jnp.where(low, swap(even), odd).astype(BF)

    out_ref[0] = jnp.dot(att_ref[...], w_ref[...], preferred_element_type=F32).astype(BF)


def split2(x):
    hi = x.astype(BF)
    return hi, (x - hi.astype(F32)).astype(BF)


def stream_kernel(
    scal_ref, term_ref, hid_ref, gate_ref, shift_ref, scale_ref, w_ref, hid_out, msg_ref
):
    first_len, base = scal_ref[0], scal_ref[4]
    projected = term_ref[0].astype(F32)
    for j in range(1, NHEAD):
        projected += term_ref[j].astype(F32)
    pos = base + lax.broadcasted_iota(jnp.int32, (TOK, 384), 0)
    first, second = pos < first_len, pos < LEN_ALL

    def per_row(table_ref):
        table = table_ref[...].astype(F32)
        return jnp.where(first, table[0:1], jnp.where(second, table[1:2], 0.0))

    x = (hid_ref[...].astype(F32) + per_row(gate_ref) * projected).astype(BF)
    hid_out[...] = x
    xf = x.astype(F32)
    total = jnp.sum(xf, axis=1, keepdims=True)
    squares = jnp.sum(xf * xf, axis=1, keepdims=True)
    x_hi, x_lo = split2(xf * (1.0 + per_row(scale_ref)))
    factor = 1.0 + scale_ref[...].astype(F32)
    f_hi, f_lo = split2(factor)
    small = jnp.concatenate(
        [f_hi.astype(F32), f_lo.astype(F32), shift_ref[...].astype(F32), jnp.zeros((10, 384), F32)], axis=0
    ).astype(BF)
    w = jnp.concatenate([w_ref[...], jnp.zeros((384, 64), BF)], axis=1)
    a = jnp.dot(x_hi, w, preferred_element_type=F32) + jnp.dot(x_lo, w, preferred_element_type=F32)
    lane = lax.broadcasted_iota(jnp.int32, (TOK, 128), 1)
    a = jnp.where(lane == 64, total, jnp.where(lane == 65, squares, a))
    b = jnp.dot(small, w, preferred_element_type=F32)
    rows8 = lax.broadcasted_iota(jnp.int32, (8, 128), 0)
    tail = jnp.where(
        rows8 == 0,
        b[0:1] + b[2:3],
        jnp.where(
            rows8 == 1,
            b[1:2] + b[3:4],
            jnp.where(rows8 == 2, b[4:5], jnp.where(rows8 == 3, b[5:6], 0.0)),
        ),
    )
    for j in range(NHEAD):
        msg_ref[j, :TOK, :] = a
        msg_ref[j, TOK:, :] = tail


def step_kernel(scal_ref, coef_ref, msg_ref, lat_ref, clean_ref, prev_ref, rim_ref):
    first_len, base, core = scal_ref[0], scal_ref[4], scal_ref[5]
    total = msg_ref[0]
    for j in range(1, NHEAD):
        total += msg_ref[j]
    pos = base + lax.broadcasted_iota(jnp.int32, (TOK, 128), 0)
    first, live = pos < first_len, pos < LEN_ALL
    mean = total[:TOK, 64:65] * (1.0 / D)
    var = total[:TOK, 65:66] * (1.0 / D) - mean * mean
    scale_w = jnp.where(first, total[TOK : TOK + 1], total[TOK + 1 : TOK + 2])
    shift_w = jnp.where(first, total[TOK + 2 : TOK + 3], total[TOK + 3 : TOK + 4])
    velocity = lax.rsqrt(var + EPSILON) * (total[:TOK] - mean * scale_w) + shift_w
    velocity = velocity[:, :64]
    first, live = first[:, :64], live[:, :64]
    latent = lat_ref[...]

    def row_coef(i):
        return jnp.where(first, coef_ref[2 * i], coef_ref[2 * i + 1])

    root_a, root_1a, root_q, root_1q = (row_coef(i) for i in range(4))
    clean = root_a * latent - root_1a * velocity
    noise = root_1a * latent + root_a * velocity
    stepped = root_q * clean + root_1q * noise
    stepped = jnp.where(live, stepped, 0.0)
    clean_ref[...] = jnp.where(live, clean, 0.0)
    prev_ref[...] = stepped
    rim_ref[...] = jnp.where(core == 0, stepped[HALF:], stepped[:HALF])


def alpha_table():
    betas = np.linspace(0.00085**0.5, 0.012**0.5, TRAIN_STEPS) ** 2
    return np.cumprod(1.0 - betas).astype(np.float32)


def request_of(position, first_len):
    return jnp.where(
        position < 0, -1, jnp.where(position < first_len, 0, jnp.where(position < LEN_ALL, 1, 2))
    )


def whole(*shape):
    return pl.BlockSpec(shape, lambda *_: (0,) * len(shape))


def shards(
    lengths,
    step_index,
    query_act,
    key_act,
    value_act,
    hidden,
    attn_weight,
    gate_mod,
    shift_mod,
    scale_mod,
    proj_weight,
    latent,
):
    z = lax.axis_index("z")
    y = lax.axis_index("y")
    core = lax.axis_index("core")
    seq = y * NZ + z
    first_len = lengths[0]
    size = jnp.where(z < 12, 32, 48)
    part = jnp.where(z < 12, z % 3, z % 2)
    scal = jnp.stack(
        [first_len, y, size, part * size, seq * TOK, core, z, seq * 0]
    ).astype(jnp.int32)
    in_smem = pl.BlockSpec(memory_space=SMEM)
    big = pltpu.CompilerParams(vmem_limit_bytes=48 * 1024 * 1024)

    packed = pl.pallas_call(
        pack_kernel, out_shape=jax.ShapeDtypeStruct((NZ, TOK, 128), BF), name="pack"
    )(query_act, key_act, value_act)
    mine = lax.all_to_all(packed, "z", 0, 0, tiled=True)
    kv = lax.all_gather(mine[:, HALF:, :].reshape(NZ * HALF, 128), "y", axis=0, tiled=True)
    partial = pl.pallas_call(
        attend_kernel,
        out_shape=jax.ShapeDtypeStruct((NZ, 64, 128), BF),
        in_specs=[in_smem, pl.BlockSpec(memory_space=VMEM), pl.BlockSpec(memory_space=VMEM)],
        out_specs=pl.BlockSpec(memory_space=VMEM),
        scratch_shapes=[
            VMEM((NY * KT, 256), BF),
            VMEM((NY * KT, 256), BF),
            VMEM((NY * KT, 128), BF),
            VMEM((NY * KT, 128), BF),
        ],
        compiler_params=big,
        name="attend",
    )(scal, mine, kv)
    parts = lax.all_to_all(partial, "z", 0, 0, tiled=True)
    term = pl.pallas_call(
        merge_kernel,
        grid=(NHEAD,),
        out_shape=jax.ShapeDtypeStruct((NHEAD, TOK, 384), BF),
        in_specs=[whole(NZ, 64, 128), pl.BlockSpec((384, 384), lambda j: (0, j))],
        out_specs=pl.BlockSpec((1, TOK, 384), lambda j: (j, 0, 0)),
        scratch_shapes=[VMEM((TOK, 384), BF)],
        name="merge",
    )(parts, attn_weight)
    terms = lax.all_to_all(term, ("x", "core"), 0, 0, tiled=True)
    hidden_out, message = pl.pallas_call(
        stream_kernel,
        out_shape=(
            jax.ShapeDtypeStruct((TOK, 384), BF),
            jax.ShapeDtypeStruct((NHEAD, TOK + 8, 128), F32),
        ),
        in_specs=[in_smem] + [pl.BlockSpec(memory_space=VMEM)] * 6,
        name="stream",
    )(scal, terms, hidden, gate_mod, shift_mod, scale_mod, proj_weight)
    message = lax.all_to_all(message, ("x", "core"), 0, 0, tiled=True)
    table = jnp.asarray(alpha_table())
    alpha_now = table[step_index]
    alpha_prev = table[step_index - STEP_GAP]
    coef = jnp.concatenate(
        [
            jnp.sqrt(alpha_now),
            jnp.sqrt(1.0 - alpha_now),
            jnp.sqrt(alpha_prev),
            jnp.sqrt(1.0 - alpha_prev),
        ]
    )
    clean, stepped, rim = pl.pallas_call(
        step_kernel,
        out_shape=(
            jax.ShapeDtypeStruct((TOK, 64), F32),
            jax.ShapeDtypeStruct((TOK, 64), F32),
            jax.ShapeDtypeStruct((HALF, 64), F32),
        ),
        in_specs=[in_smem, in_smem] + [pl.BlockSpec(memory_space=VMEM)] * 2,
        name="ddim",
    )(scal, coef, message, latent)
    pairs = []
    for s in range(NY * NZ):
        for x in range(NX):
            up, down = (s * NX + x) * NC, (s * NX + x) * NC + 1
            if s + 1 < NY * NZ:
                pairs.append((up, up + NX * NC))
            if s > 0:
                pairs.append((down, down - NX * NC))
    got = lax.ppermute(rim, ("y", "z", "x", "core"), pairs)
    both = lax.all_gather(got, "core")
    offsets = jnp.arange(RIM, dtype=jnp.int32)
    start = seq * TOK
    lower_ok = request_of(start - RIM + offsets, first_len) == request_of(start, first_len)
    upper_ok = request_of(start + TOK + offsets, first_len) == request_of(
        start + TOK - 1, first_len
    )
    lower_ok &= start > 0
    upper_ok &= start + TOK < NY * NZ * TOK
    rims = jnp.concatenate(
        [
            jnp.where(lower_ok[:, None], both[0, HALF - RIM :], 0.0),
            jnp.where(upper_ok[:, None], both[1, :RIM], 0.0),
        ],
        axis=0,
    )
    return hidden_out, clean, stepped, rims


def solution(mesh):
    grid = Mesh(mesh.devices.reshape(NY, NZ, NX, NC), ("y", "z", "x", "core"))
    seq, head = ("y", "z"), ("x", "core")
    in_specs = (
        P(),
        P(),
        P(seq, head),
        P(seq, head),
        P(seq, head),
        P(seq, head),
        P(head, None),
        P(None, head),
        P(None, head),
        P(None, head),
        P(head, None),
        P(seq, None),
    )
    out_specs = (P(seq, head), P(seq, None), P(seq, None), P(seq, None))
    return jax.shard_map(shards, mesh=grid, in_specs=in_specs, out_specs=out_specs, check_vma=False)
```

```python
import jax
import jax.numpy as jnp
import numpy as np
from jax import lax
from jax.experimental import pallas as pl
from jax.experimental.pallas import tpu as pltpu
from jax.sharding import Mesh
from jax.sharding import PartitionSpec as P

D = 3072
HD = 64
RIM = 45
TOK = 96
HALF = 48
LEN_ALL = 5952
TRAIN_STEPS = 1000
STEP_GAP = 20
NY, NZ, NX, NC = 4, 16, 4, 2
NHEAD = 8
EPSILON = 1e-06
MASKED = -1e30
FLOOR = -0.5e30
HEAD_OF = (0, 0, 0, 1, 1, 1, 2, 2, 2, 3, 3, 3, 4, 4, 5, 5)
PART_OF = (0, 1, 2, 0, 1, 2, 0, 1, 2, 0, 1, 2, 0, 1, 0, 1)
SIZE_OF = (32,) * 12 + (48,) * 4
BF = jnp.bfloat16
F32 = jnp.float32
SMEM = pltpu.SMEM
VMEM = pltpu.VMEM


def low_lanes(rows):
    return lax.broadcasted_iota(jnp.int32, (rows, 128), 1) < HD


def swap(x):
    return pltpu.roll(x, HD, 1)


def pack_kernel(q_ref, k_ref, v_ref, queries_ref, keyvals_ref):
    low_h, low_t = low_lanes(HALF), low_lanes(TOK)
    for pair in range(3):
        lanes = slice(128 * pair, 128 * pair + 128)
        q = q_ref[:, lanes].astype(F32) * 0.125
        k = k_ref[:, lanes].astype(F32)
        v = v_ref[:, lanes].astype(F32)
        top, bottom = q[:HALF], q[HALF:]
        queries = (jnp.where(low_h, top, swap(bottom)), jnp.where(low_h, swap(top), bottom))
        keyvals = (jnp.where(low_t, k, swap(v)), jnp.where(low_t, swap(k), v))
        for side in range(2):
            qh = queries[side].astype(BF)
            kvh = keyvals[side].astype(BF)
            for d in range(NZ):
                if HEAD_OF[d] != 2 * pair + side:
                    continue
                size = SIZE_OF[d]
                start = PART_OF[d] * size
                queries_ref[d] = qh
                keyvals_ref[d, :size, :] = kvh[start : start + size]
                if size < HALF:
                    keyvals_ref[d, size:, :] = jnp.zeros((HALF - size, 128), BF)


def pieces(x):
    hi = x.astype(BF).astype(F32)
    rest = x - hi
    mid = rest.astype(BF).astype(F32)
    return (hi, mid, rest - mid)


QT = 384
KT = 768
HALVES = NZ * HALF
TILES = 2 * HALVES // QT
ONES = 131


def attend_kernel(scal_ref, q_ref, kv_ref, out_ref, key_ref, query_ref, top_ref, acc_ref):
    first_len, row, size, offset = scal_ref[0], scal_ref[1], scal_ref[2], scal_ref[3]
    lane3 = lax.broadcasted_iota(jnp.int32, (NZ, HALF, 128), 2)
    slot = lax.broadcasted_iota(jnp.int32, (NZ, HALF, 128), 1)
    block = lax.broadcasted_iota(jnp.int32, (NZ, HALF, 128), 0) * TOK + slot
    for j in range(NY):
        pos = jnp.where(slot < size, block + (j * NZ * TOK + offset), LEN_ALL)
        own = jnp.where(pos < first_len, 0, jnp.where(pos < LEN_ALL, 1, -1))
        extra = jnp.where((lane3 < 3) & (lane3 != own), MASKED, 0.0)
        extra = jnp.where(lane3 == ONES - 128, 1.0, extra)
        key_ref[j, :, :128] = kv_ref[j * KT : (j + 1) * KT, :]
        key_ref[j, :, 128:] = extra.reshape(KT, 128).astype(BF)

    low = low_lanes(HALVES)
    q = q_ref[...].astype(F32).reshape(HALVES, 128)
    for side in range(2):
        pos = block + (row * NZ * TOK + side * HALF)
        own = jnp.where(pos < first_len, 0, jnp.where(pos < LEN_ALL, 1, 2))
        extra = jnp.where(lane3 == own, 1.0, 0.0).reshape(HALVES, 128)
        rows = slice(side * HALVES, (side + 1) * HALVES)
        query_ref[rows, :128] = jnp.where(low, swap(q) if side else q, 0.0).astype(BF)
        query_ref[rows, 128:] = extra.astype(BF)
    top_ref[...] = jnp.full_like(top_ref, FLOOR)
    acc_ref[...] = jnp.zeros_like(acc_ref)

    def holds(start, stop):
        stop = jnp.minimum(stop, LEN_ALL)
        return start < first_len, (stop > first_len) & (start < stop)

    def visit(number, carry):
        j, tile = number // TILES, number % TILES
        start = row * (NZ * TOK) + (tile % (TILES // 2)) * (QT // HALF * TOK)
        q_first, q_second = holds(start, start + QT // HALF * TOK)
        k_first, k_second = holds(j * (NZ * TOK), (j + 1) * (NZ * TOK))

        @pl.when((q_first & k_first) | (q_second & k_second))
        def _():
            rows = pl.ds(tile * QT, QT)
            keys = key_ref[j]
            scores = lax.dot_general(
                query_ref[rows, :], keys, (((1,), (1,)), ((), ())), preferred_element_type=F32
            )
            old = top_ref[rows, :1]
            new = jnp.maximum(jnp.max(scores, axis=1, keepdims=True), old)
            weights = jnp.exp(scores - new).astype(BF)
            acc_ref[rows, :] = acc_ref[rows, :] * jnp.exp(old - new) + jnp.dot(
                weights, keys, preferred_element_type=F32
            )
            top_ref[rows, :] = jnp.broadcast_to(new, (QT, 128))

        return carry

    lax.fori_loop(0, NY * TILES, visit, 0)

    lane = lax.broadcasted_iota(jnp.int32, (HALVES, 128), 1)
    eye = (
        lax.broadcasted_iota(jnp.int32, (TOK, 128), 0)
        == lax.broadcasted_iota(jnp.int32, (TOK, 128), 1)
    ).astype(BF)
    outs, stats = [], []
    for side in range(2):
        rows = slice(side * HALVES, (side + 1) * HALVES)
        sums = acc_ref[rows, ONES : ONES + 1]
        outs.append(acc_ref[rows, :128] / jnp.where(sums > 0.0, sums, 1.0))
        stat = jnp.zeros((HALVES, 128), F32)
        for number, piece in enumerate(pieces(top_ref[rows, :1]) + pieces(sums)):
            stat = jnp.where(lane == number, piece, stat)
        stats.append(stat.astype(BF))
    mixed = jnp.where(low, swap(outs[0]), outs[1]).astype(BF)
    for b in range(NZ):
        rows = slice(b * HALF, (b + 1) * HALF)
        out_ref[b, :HALF, :] = mixed[rows]
        both = jnp.concatenate([stats[0][rows], stats[1][rows]], axis=0)
        turned = lax.dot_general(
            both, eye, (((0,), (0,)), ((), ())), preferred_element_type=F32
        )
        out_ref[b, HALF:, :] = turned[:8].astype(BF)


def merge_kernel(part_ref, w_ref, out_ref, att_ref, copy_ref, sem):
    copy = pltpu.make_async_copy(w_ref, copy_ref, sem)
    copy.start()
    low = low_lanes(HALF)
    stat = part_ref[:, HALF:, :].astype(F32)
    tops = stat[:, 0] + stat[:, 1] + stat[:, 2]
    sums = stat[:, 3] + stat[:, 4] + stat[:, 5]
    shares = []
    for h in range(6):
        own = [d for d in range(NZ) if HEAD_OF[d] == h]
        rows = slice(own[0], own[-1] + 1)
        top = jnp.max(tops[rows], axis=0, keepdims=True)
        scaled = jnp.exp(tops[rows] - top) * sums[rows]
        total = jnp.sum(scaled, axis=0, keepdims=True)
        shares.append(scaled / jnp.where(total > 0.0, total, 1.0))
    shares = jnp.concatenate(shares + [jnp.zeros((128 - NZ, 128), F32)], axis=0).T
    heads = []
    for h in range(6):
        mixed = jnp.zeros((HALF, 128), F32)
        for d in range(NZ):
            if HEAD_OF[d] == h:
                weight = jnp.where(
                    low, shares[:HALF, d : d + 1], shares[HALF : 2 * HALF, d : d + 1]
                )
                mixed += weight * part_ref[d, :HALF, :].astype(F32)
        heads.append(mixed)
    for pair in range(3):
        even, odd = heads[2 * pair], heads[2 * pair + 1]
        lanes = slice(128 * pair, 128 * pair + 128)
        att_ref[:HALF, lanes] = jnp.where(low, even, swap(odd)).astype(BF)
        att_ref[HALF:, lanes] = jnp.where(low, swap(even), odd).astype(BF)
    copy.wait()
    for j in range(NHEAD):
        out_ref[j] = jnp.dot(
            att_ref[...], copy_ref[:, 384 * j : 384 * j + 384], preferred_element_type=F32
        ).astype(BF)


def split2(x):
    hi = x.astype(BF)
    return hi, (x - hi.astype(F32)).astype(BF)


def stream_kernel(
    scal_ref, term_ref, hid_ref, gate_ref, shift_ref, scale_ref, w_ref, hid_out, msg_ref
):
    first_len, base = scal_ref[0], scal_ref[4]
    projected = term_ref[0].astype(F32)
    for j in range(1, NHEAD):
        projected += term_ref[j].astype(F32)
    pos = base + lax.broadcasted_iota(jnp.int32, (TOK, 384), 0)
    first, second = pos < first_len, pos < LEN_ALL

    def per_row(table):
        return jnp.where(first, table[0:1], jnp.where(second, table[1:2], 0.0))

    gate, shift = gate_ref[...].astype(F32), shift_ref[...].astype(F32)
    factor = 1.0 + scale_ref[...].astype(F32)
    x = (hid_ref[...].astype(F32) + per_row(gate) * projected).astype(BF)
    hid_out[...] = x
    xf = x.astype(F32)
    scaled = jnp.concatenate(
        [xf * per_row(factor), factor, shift, jnp.zeros((28, 384), F32)], axis=0
    )
    sq_hi, sq_lo = split2(xf * xf)
    ones = jnp.ones((8, 384), BF)

    def turn(left, right):
        return lax.dot_general(left, right, (((1,), (1,)), ((), ())), preferred_element_type=F32)

    high, rest = split2(scaled)
    w = w_ref[...]
    a = turn(w, high) + turn(w, rest)
    total = turn(ones, x)
    squares = turn(ones, sq_hi) + turn(ones, sq_lo)
    rows8 = lax.broadcasted_iota(jnp.int32, (8, TOK), 0)
    tail = jnp.where(rows8 == 0, total, squares)
    for j in range(NHEAD):
        msg_ref[j, :64, :] = a
        msg_ref[j, 64:, :TOK] = tail
        msg_ref[j, 64:, TOK:] = jnp.zeros((8, 128 - TOK), F32)


def step_kernel(scal_ref, coef_ref, msg_ref, lat_ref, clean_ref, prev_ref):
    first_len, base = scal_ref[0], scal_ref[4]
    total = msg_ref[0]
    for j in range(1, NHEAD):
        total += msg_ref[j]
    pos = base + lax.broadcasted_iota(jnp.int32, (64, TOK), 1)
    first, live = pos < first_len, pos < LEN_ALL
    mean = total[64:65, :TOK] * (1.0 / D)
    var = total[65:66, :TOK] * (1.0 / D) - mean * mean
    scale_w = jnp.where(first, total[:64, TOK : TOK + 1], total[:64, TOK + 1 : TOK + 2])
    shift_w = jnp.where(first, total[:64, TOK + 2 : TOK + 3], total[:64, TOK + 3 : TOK + 4])
    velocity = lax.rsqrt(var + EPSILON) * (total[:64, :TOK] - mean * scale_w) + shift_w
    latent = lat_ref[...]

    def row_coef(i):
        return jnp.where(first, coef_ref[2 * i], coef_ref[2 * i + 1])

    root_a, root_1a, root_q, root_1q = (row_coef(i) for i in range(4))
    clean = root_a * latent - root_1a * velocity
    noise = root_1a * latent + root_a * velocity
    stepped = root_q * clean + root_1q * noise
    clean_ref[...] = jnp.where(live, clean, 0.0)
    prev_ref[...] = jnp.where(live, stepped, 0.0)


def alpha_table():
    betas = np.linspace(0.00085**0.5, 0.012**0.5, TRAIN_STEPS) ** 2
    return np.cumprod(1.0 - betas).astype(np.float32)


def request_of(position, first_len):
    return jnp.where(
        position < 0, -1, jnp.where(position < first_len, 0, jnp.where(position < LEN_ALL, 1, 2))
    )


def shards(
    lengths,
    step_index,
    query_act,
    key_act,
    value_act,
    hidden,
    attn_weight,
    gate_mod,
    shift_mod,
    scale_mod,
    proj_weight,
    latent,
):
    z = lax.axis_index("z")
    y = lax.axis_index("y")
    seq = y * NZ + z
    first_len = lengths[0]
    size = jnp.where(z < 12, 32, 48)
    part = jnp.where(z < 12, z % 3, z % 2)
    scal = jnp.stack([first_len, y, size, part * size, seq * TOK]).astype(jnp.int32)
    in_smem = pl.BlockSpec(memory_space=SMEM)
    big = pltpu.CompilerParams(vmem_limit_bytes=48 * 1024 * 1024)

    any_vmem = pl.BlockSpec(memory_space=VMEM)

    queries, keyvals = pl.pallas_call(
        pack_kernel,
        out_shape=(jax.ShapeDtypeStruct((NZ, HALF, 128), BF),) * 2,
        name="pack",
    )(query_act, key_act, value_act)
    keyvals = lax.all_to_all(keyvals, "z", 0, 0, tiled=True)
    keyvals, queries = lax.optimization_barrier((keyvals, queries))
    queries = lax.all_to_all(queries, "z", 0, 0, tiled=True)
    keyvals = lax.all_gather(keyvals.reshape(NZ * HALF, 128), "y", axis=0, tiled=True)
    partial = pl.pallas_call(
        attend_kernel,
        out_shape=jax.ShapeDtypeStruct((NZ, HALF + 8, 128), BF),
        in_specs=[in_smem, any_vmem, any_vmem],
        out_specs=any_vmem,
        scratch_shapes=[
            VMEM((NY, KT, 256), BF),
            VMEM((2 * HALVES, 256), BF),
            VMEM((2 * HALVES, 128), F32),
            VMEM((2 * HALVES, 256), F32),
        ],
        compiler_params=big,
        name="attend",
    )(scal, queries, keyvals)
    parts = lax.all_to_all(partial, "z", 0, 0, tiled=True)
    term = pl.pallas_call(
        merge_kernel,
        out_shape=jax.ShapeDtypeStruct((NHEAD, TOK, 384), BF),
        in_specs=[any_vmem, pl.BlockSpec(memory_space=pl.ANY)],
        out_specs=any_vmem,
        scratch_shapes=[VMEM((TOK, 384), BF), VMEM((384, D), BF), pltpu.SemaphoreType.DMA],
        compiler_params=big,
        name="merge",
    )(parts, attn_weight)
    terms = lax.all_to_all(term, ("x", "core"), 0, 0, tiled=True)
    hidden_out, message = pl.pallas_call(
        stream_kernel,
        out_shape=(
            jax.ShapeDtypeStruct((TOK, 384), BF),
            jax.ShapeDtypeStruct((NHEAD, 72, 128), F32),
        ),
        in_specs=[in_smem] + [any_vmem] * 6,
        name="stream",
    )(scal, terms, hidden, gate_mod, shift_mod, scale_mod, proj_weight.T)
    message = lax.all_to_all(message, ("x", "core"), 0, 0, tiled=True)
    table = jnp.asarray(alpha_table())
    alpha_now = table[step_index]
    alpha_prev = table[step_index - STEP_GAP]
    coef = jnp.concatenate(
        [
            jnp.sqrt(alpha_now),
            jnp.sqrt(1.0 - alpha_now),
            jnp.sqrt(alpha_prev),
            jnp.sqrt(1.0 - alpha_prev),
        ]
    )
    clean, stepped = pl.pallas_call(
        step_kernel,
        out_shape=(jax.ShapeDtypeStruct((64, TOK), F32),) * 2,
        in_specs=[in_smem, in_smem, any_vmem, any_vmem],
        name="ddim",
    )(scal, coef, message, latent.T)
    pairs = []
    for s in range(NY * NZ):
        for x in range(NX):
            up, down = (s * NX + x) * NC, (s * NX + x) * NC + 1
            if s + 1 < NY * NZ:
                pairs.append((up, up + NX * NC))
            if s > 0:
                pairs.append((down, down - NX * NC))
    got = lax.ppermute(stepped, ("y", "z", "x", "core"), pairs)
    both = lax.all_gather(got, "core")
    offsets = jnp.arange(RIM, dtype=jnp.int32)
    start = seq * TOK
    lower_ok = request_of(start - RIM + offsets, first_len) == request_of(start, first_len)
    upper_ok = request_of(start + TOK + offsets, first_len) == request_of(
        start + TOK - 1, first_len
    )
    lower_ok &= start > 0
    upper_ok &= start + TOK < NY * NZ * TOK
    rims = jnp.concatenate(
        [
            jnp.where(lower_ok[None], both[0, :, TOK - RIM :], 0.0),
            jnp.where(upper_ok[None], both[1, :, :RIM], 0.0),
        ],
        axis=1,
    )
    return hidden_out, clean.T, stepped.T, rims.T


def solution(mesh):
    grid = Mesh(mesh.devices.reshape(NY, NZ, NX, NC), ("y", "z", "x", "core"))
    seq, head = ("y", "z"), ("x", "core")
    in_specs = (
        P(),
        P(),
        P(seq, head),
        P(seq, head),
        P(seq, head),
        P(seq, head),
        P(head, None),
        P(None, head),
        P(None, head),
        P(None, head),
        P(head, None),
        P(seq, None),
    )
    out_specs = (P(seq, head), P(seq, None), P(seq, None), P(seq, None))
    return jax.shard_map(shards, mesh=grid, in_specs=in_specs, out_specs=out_specs, check_vma=False)
```

```python
import jax
import jax.numpy as jnp
import numpy as np
from jax import lax
from jax.experimental import pallas as pl
from jax.experimental.pallas import tpu as pltpu
from jax.sharding import Mesh
from jax.sharding import PartitionSpec as P

D = 3072
HD = 64
RIM = 45
TOK = 96
HALF = 48
LEN_ALL = 5952
TRAIN_STEPS = 1000
STEP_GAP = 20
NY, NA, NB, NX, NC = 4, 4, 4, 4, 2
NG = NY * NB
NHEAD = 8
EPSILON = 1e-06
MASKED = -1e30
FLOOR = -0.5e30
HEAD_OF = (0, 0, 0, 1, 1, 1, 2, 2, 2, 3, 3, 3, 4, 4, 5, 5)
PART_OF = (0, 1, 2, 0, 1, 2, 0, 1, 2, 0, 1, 2, 0, 1, 0, 1)
SIZE_OF = (32,) * 12 + (48,) * 4
BF = jnp.bfloat16
F32 = jnp.float32
SMEM = pltpu.SMEM
VMEM = pltpu.VMEM


def low_lanes(rows):
    return lax.broadcasted_iota(jnp.int32, (rows, 128), 1) < HD


def swap(x):
    return pltpu.roll(x, HD, 1)


def pack_kernel(q_ref, k_ref, v_ref, out_ref):
    low_h, low_t = low_lanes(HALF), low_lanes(TOK)
    for pair in range(3):
        lanes = slice(128 * pair, 128 * pair + 128)
        q = q_ref[:, lanes].astype(F32) * 0.125
        k = k_ref[:, lanes].astype(F32)
        v = v_ref[:, lanes].astype(F32)
        top, bottom = q[:HALF], q[HALF:]
        queries = (jnp.where(low_h, top, swap(bottom)), jnp.where(low_h, swap(top), bottom))
        keyvals = (jnp.where(low_t, k, swap(v)), jnp.where(low_t, swap(k), v))
        for side in range(2):
            qh = queries[side].astype(BF)
            kvh = keyvals[side].astype(BF)
            for d in range(NG):
                if HEAD_OF[d] != 2 * pair + side:
                    continue
                size = SIZE_OF[d]
                start = PART_OF[d] * size
                out_ref[d, :HALF, :] = qh
                out_ref[d, HALF : HALF + size, :] = kvh[start : start + size]
                if size < HALF:
                    out_ref[d, HALF + size :, :] = jnp.zeros((HALF - size, 128), BF)


def pieces(x):
    hi = x.astype(BF).astype(F32)
    rest = x - hi
    mid = rest.astype(BF).astype(F32)
    return (hi, mid, rest - mid)


QT = NB * TOK
KT = NA * NB * HALF
ROWS = 80


def attend_kernel(scal_ref, q_ref, kv_ref, out_ref, key_ref, val_ref, query_ref, top_ref, acc_ref):
    first_len, column, size, offset = scal_ref[0], scal_ref[1], scal_ref[2], scal_ref[3]
    row_tok = NA * NB * TOK
    lane3 = lax.broadcasted_iota(jnp.int32, (NA * NB, HALF, 128), 2)
    slot = lax.broadcasted_iota(jnp.int32, (NA * NB, HALF, 128), 1)
    block = lax.broadcasted_iota(jnp.int32, (NA * NB, HALF, 128), 0) * TOK + slot
    low = low_lanes(HALF)
    lane_q = lax.broadcasted_iota(jnp.int32, (16, QT), 1)
    row_q = lax.broadcasted_iota(jnp.int32, (16, QT), 0)
    part = NB * HALF
    ones = (lax.broadcasted_iota(jnp.int32, (ROWS - HD, KT), 0) == 0).astype(F32)
    for j in range(NY):
        pos = jnp.where(slot < size, block + (j * row_tok + offset), LEN_ALL)
        own = jnp.where(pos < first_len, 0, jnp.where(pos < LEN_ALL, 1, -1))
        extra = jnp.where((lane3 < 3) & (lane3 != own), MASKED, 0.0)
        key_ref[j, :, 128:] = extra.reshape(KT, 128).astype(BF)
        for i in range(NA):
            rows = slice(i * part, (i + 1) * part)
            start = (i * NY + j) * part
            key_ref[j, rows, :128] = kv_ref[start : start + part, :]
        turned = key_ref[j, :, :128].astype(F32).T
        val_ref[j] = jnp.concatenate([turned[HD:], ones], axis=0).astype(BF)

        stack = []
        for c in range(NB):
            q = q_ref[j * NB + c, :HALF, :].astype(F32)
            stack += [jnp.where(low, q, 0.0), jnp.where(low, swap(q), 0.0)]
        query_ref[j, :128, :] = jnp.concatenate(stack, axis=0).T.astype(BF)
        pos = lane_q + (j * row_tok + column * QT)
        own = jnp.where(pos < first_len, 0, jnp.where(pos < LEN_ALL, 1, 2))
        query_ref[j, 128:144, :] = jnp.where(row_q == own, 1.0, 0.0).astype(BF)
        query_ref[j, 144:, :] = jnp.zeros((112, QT), BF)
    top_ref[...] = jnp.full_like(top_ref, FLOOR)
    acc_ref[...] = jnp.zeros_like(acc_ref)

    def holds(start, stop):
        stop = jnp.minimum(stop, LEN_ALL)
        return start < first_len, (stop > first_len) & (start < stop)

    def visit(number, carry):
        j, t = number // NY, number % NY
        start = t * row_tok + column * QT
        q_first, q_second = holds(start, start + QT)
        k_first, k_second = holds(j * row_tok, (j + 1) * row_tok)

        @pl.when((q_first & k_first) | (q_second & k_second))
        def _():
            scores = jnp.dot(key_ref[j], query_ref[t], preferred_element_type=F32)
            old = top_ref[t, :1, :]
            new = jnp.maximum(jnp.max(scores, axis=0, keepdims=True), old)
            weights = jnp.exp(scores - new).astype(BF)
            acc_ref[t] = acc_ref[t] * jnp.exp(old - new) + jnp.dot(
                val_ref[j], weights, preferred_element_type=F32
            )
            top_ref[t] = jnp.broadcast_to(new, (8, QT))

        return carry

    lax.fori_loop(0, NY * NY, visit, 0)

    row8 = lax.broadcasted_iota(jnp.int32, (8, QT), 0)
    for t in range(NY):
        sums = acc_ref[t, HD : HD + 1, :]
        stats = jnp.zeros((8, QT), F32)
        for number, piece in enumerate(pieces(top_ref[t, :1, :]) + pieces(sums)):
            stats = jnp.where(row8 == number, piece, stats)
        whole = jnp.concatenate(
            [acc_ref[t, :HD, :] * (1.0 / jnp.where(sums > 0.0, sums, 1.0)), stats], axis=0
        )
        for c in range(NB):
            moved = pltpu.roll(whole, QT - c * TOK, 1) if c else whole
            out_ref[t * NB + c] = moved[:, :128].astype(BF)


def merge_kernel(part_ref, w_ref, out_ref, att_ref, copy_ref, sem):
    copy = pltpu.make_async_copy(w_ref, copy_ref, sem)
    copy.start()
    stat = part_ref[:, HD:, :].astype(F32)
    tops = stat[:, 0] + stat[:, 1] + stat[:, 2]
    sums = stat[:, 3] + stat[:, 4] + stat[:, 5]
    for h in range(6):
        own = [d for d in range(NG) if HEAD_OF[d] == h]
        rows = slice(own[0], own[-1] + 1)
        top = jnp.max(tops[rows], axis=0, keepdims=True)
        scaled = jnp.exp(tops[rows] - top) * sums[rows]
        total = jnp.sum(scaled, axis=0, keepdims=True)
        shares = scaled / jnp.where(total > 0.0, total, 1.0)
        mixed = jnp.zeros((HD, 128), F32)
        for i, d in enumerate(own):
            mixed += shares[i : i + 1] * part_ref[d, :HD, :].astype(F32)
        att_ref[HD * h : HD * h + HD, :] = mixed
    attended = att_ref[...].T[:TOK].astype(BF)
    copy.wait()
    for j in range(NHEAD):
        out_ref[j] = jnp.dot(
            attended, copy_ref[:, 384 * j : 384 * j + 384], preferred_element_type=F32
        ).astype(BF)


def split2(x):
    hi = x.astype(BF)
    return hi, (x - hi.astype(F32)).astype(BF)


def stream_kernel(
    scal_ref, term_ref, hid_ref, gate_ref, shift_ref, scale_ref, w_ref, hid_out, msg_ref
):
    first_len, base = scal_ref[0], scal_ref[4]
    projected = term_ref[0].astype(F32)
    for j in range(1, NHEAD):
        projected += term_ref[j].astype(F32)
    pos = base + lax.broadcasted_iota(jnp.int32, (TOK, 384), 0)
    first, second = pos < first_len, pos < LEN_ALL

    def per_row(table):
        return jnp.where(first, table[0:1], jnp.where(second, table[1:2], 0.0))

    gate, shift = gate_ref[...].astype(F32), shift_ref[...].astype(F32)
    factor = 1.0 + scale_ref[...].astype(F32)
    x = (hid_ref[...].astype(F32) + per_row(gate) * projected).astype(BF)
    hid_out[...] = x
    xf = x.astype(F32)
    scaled = jnp.concatenate(
        [xf * per_row(factor), factor, shift, jnp.zeros((28, 384), F32)], axis=0
    )
    sq_hi, sq_lo = split2(xf * xf)
    ones = jnp.ones((8, 384), BF)

    def turn(left, right):
        return lax.dot_general(left, right, (((1,), (1,)), ((), ())), preferred_element_type=F32)

    high, rest = split2(scaled)
    w = w_ref[...]
    a = turn(w, high) + turn(w, rest)
    total = turn(ones, x)
    squares = turn(ones, sq_hi) + turn(ones, sq_lo)
    rows8 = lax.broadcasted_iota(jnp.int32, (8, TOK), 0)
    tail = jnp.where(rows8 == 0, total, squares)
    for j in range(NHEAD):
        msg_ref[j, :64, :] = a
        msg_ref[j, 64:, :TOK] = tail
        msg_ref[j, 64:, TOK:] = jnp.zeros((8, 128 - TOK), F32)


def step_kernel(scal_ref, coef_ref, msg_ref, lat_ref, clean_ref, prev_ref):
    first_len, base = scal_ref[0], scal_ref[4]
    total = msg_ref[0]
    for j in range(1, NHEAD):
        total += msg_ref[j]
    pos = base + lax.broadcasted_iota(jnp.int32, (64, TOK), 1)
    first, live = pos < first_len, pos < LEN_ALL
    mean = total[64:65, :TOK] * (1.0 / D)
    var = total[65:66, :TOK] * (1.0 / D) - mean * mean
    scale_w = jnp.where(first, total[:64, TOK : TOK + 1], total[:64, TOK + 1 : TOK + 2])
    shift_w = jnp.where(first, total[:64, TOK + 2 : TOK + 3], total[:64, TOK + 3 : TOK + 4])
    velocity = lax.rsqrt(var + EPSILON) * (total[:64, :TOK] - mean * scale_w) + shift_w
    latent = lat_ref[...]

    def row_coef(i):
        return jnp.where(first, coef_ref[2 * i], coef_ref[2 * i + 1])

    root_a, root_1a, root_q, root_1q = (row_coef(i) for i in range(4))
    clean = root_a * latent - root_1a * velocity
    noise = root_1a * latent + root_a * velocity
    stepped = root_q * clean + root_1q * noise
    clean_ref[...] = jnp.where(live, clean, 0.0)
    prev_ref[...] = jnp.where(live, stepped, 0.0)


def alpha_table():
    betas = np.linspace(0.00085**0.5, 0.012**0.5, TRAIN_STEPS) ** 2
    return np.cumprod(1.0 - betas).astype(np.float32)


def request_of(position, first_len):
    return jnp.where(
        position < 0, -1, jnp.where(position < first_len, 0, jnp.where(position < LEN_ALL, 1, 2))
    )


def shards(
    lengths,
    step_index,
    query_act,
    key_act,
    value_act,
    hidden,
    attn_weight,
    gate_mod,
    shift_mod,
    scale_mod,
    proj_weight,
    latent,
):
    y, column, c = lax.axis_index("y"), lax.axis_index("a"), lax.axis_index("c")
    seq = (y * NA + column) * NB + c
    member = y * NB + c
    first_len = lengths[0]
    size = jnp.where(member < 12, 32, 48)
    part = jnp.where(member < 12, member % 3, member % 2)
    scal = jnp.stack([first_len, column, size, part * size, seq * TOK]).astype(jnp.int32)
    in_smem = pl.BlockSpec(memory_space=SMEM)
    big = pltpu.CompilerParams(vmem_limit_bytes=48 * 1024 * 1024)

    any_vmem = pl.BlockSpec(memory_space=VMEM)

    packed = pl.pallas_call(
        pack_kernel, out_shape=jax.ShapeDtypeStruct((NG, TOK, 128), BF), name="pack"
    )(query_act, key_act, value_act)
    mine = lax.all_to_all(packed, ("y", "c"), 0, 0, tiled=True)
    keyvals = lax.all_gather(mine[:, HALF:].reshape(NG * HALF, 128), "a", axis=0, tiled=True)
    partial = pl.pallas_call(
        attend_kernel,
        out_shape=jax.ShapeDtypeStruct((NG, HD + 8, 128), BF),
        in_specs=[in_smem, any_vmem, any_vmem],
        out_specs=any_vmem,
        scratch_shapes=[
            VMEM((NY, KT, 256), BF),
            VMEM((NY, ROWS, KT), BF),
            VMEM((NY, 256, QT), BF),
            VMEM((NY, 8, QT), F32),
            VMEM((NY, ROWS, QT), F32),
        ],
        compiler_params=big,
        name="attend",
    )(scal, mine, keyvals)
    parts = lax.all_to_all(partial, ("y", "c"), 0, 0, tiled=True)
    term = pl.pallas_call(
        merge_kernel,
        out_shape=jax.ShapeDtypeStruct((NHEAD, TOK, 384), BF),
        in_specs=[any_vmem, pl.BlockSpec(memory_space=pl.ANY)],
        out_specs=any_vmem,
        scratch_shapes=[VMEM((384, 128), F32), VMEM((384, D), BF), pltpu.SemaphoreType.DMA],
        compiler_params=big,
        name="merge",
    )(parts, attn_weight)
    terms = lax.all_to_all(term, ("x", "core"), 0, 0, tiled=True)
    hidden_out, message = pl.pallas_call(
        stream_kernel,
        out_shape=(
            jax.ShapeDtypeStruct((TOK, 384), BF),
            jax.ShapeDtypeStruct((NHEAD, 72, 128), F32),
        ),
        in_specs=[in_smem] + [any_vmem] * 6,
        name="stream",
    )(scal, terms, hidden, gate_mod, shift_mod, scale_mod, proj_weight.T)
    message = lax.all_to_all(message, ("x", "core"), 0, 0, tiled=True)
    table = jnp.asarray(alpha_table())
    alpha_now = table[step_index]
    alpha_prev = table[step_index - STEP_GAP]
    coef = jnp.concatenate(
        [
            jnp.sqrt(alpha_now),
            jnp.sqrt(1.0 - alpha_now),
            jnp.sqrt(alpha_prev),
            jnp.sqrt(1.0 - alpha_prev),
        ]
    )
    clean, stepped = pl.pallas_call(
        step_kernel,
        out_shape=(jax.ShapeDtypeStruct((64, TOK), F32),) * 2,
        in_specs=[in_smem, in_smem, any_vmem, any_vmem],
        name="ddim",
    )(scal, coef, message, latent.T)
    pairs = []
    for s in range(NY * NA * NB):
        for x in range(NX):
            up, down = (s * NX + x) * NC, (s * NX + x) * NC + 1
            if s + 1 < NY * NA * NB:
                pairs.append((up, up + NX * NC))
            if s > 0:
                pairs.append((down, down - NX * NC))
    got = lax.ppermute(stepped, ("y", "a", "c", "x", "core"), pairs)
    both = lax.all_gather(got, "core")
    offsets = jnp.arange(RIM, dtype=jnp.int32)
    start = seq * TOK
    lower_ok = request_of(start - RIM + offsets, first_len) == request_of(start, first_len)
    upper_ok = request_of(start + TOK + offsets, first_len) == request_of(
        start + TOK - 1, first_len
    )
    lower_ok &= start > 0
    upper_ok &= start + TOK < NY * NA * NB * TOK
    rims = jnp.concatenate(
        [
            jnp.where(lower_ok[None], both[0, :, TOK - RIM :], 0.0),
            jnp.where(upper_ok[None], both[1, :, :RIM], 0.0),
        ],
        axis=1,
    )
    return hidden_out, clean.T, stepped.T, rims.T


def solution(mesh):
    grid = Mesh(mesh.devices.reshape(NY, NA, NB, NX, NC), ("y", "a", "c", "x", "core"))
    seq, head = ("y", "a", "c"), ("x", "core")
    in_specs = (
        P(),
        P(),
        P(seq, head),
        P(seq, head),
        P(seq, head),
        P(seq, head),
        P(head, None),
        P(None, head),
        P(None, head),
        P(None, head),
        P(head, None),
        P(seq, None),
    )
    out_specs = (P(seq, head), P(seq, None), P(seq, None), P(seq, None))
    return jax.shard_map(shards, mesh=grid, in_specs=in_specs, out_specs=out_specs, check_vma=False)
```

```python
import jax
import jax.numpy as jnp
import numpy as np
from jax import lax
from jax.experimental import pallas as pl
from jax.experimental.pallas import tpu as pltpu
from jax.sharding import Mesh
from jax.sharding import PartitionSpec as P

D = 3072
HD = 64
RIM = 45
TOK = 96
HALF = 48
LEN_ALL = 5952
TRAIN_STEPS = 1000
STEP_GAP = 20
NY, NA, NB, NX, NC = 4, 4, 4, 4, 2
NG = NY * NB
NHEAD = 8
EPSILON = 1e-06
MASKED = -1e30
FLOOR = -0.5e30
HEAD_OF = (0, 0, 0, 1, 1, 1, 2, 2, 2, 3, 3, 3, 4, 4, 5, 5)
PART_OF = (0, 1, 2, 0, 1, 2, 0, 1, 2, 0, 1, 2, 0, 1, 0, 1)
SIZE_OF = (32,) * 12 + (48,) * 4
BF = jnp.bfloat16
F32 = jnp.float32
SMEM = pltpu.SMEM
VMEM = pltpu.VMEM


def low_lanes(rows):
    return lax.broadcasted_iota(jnp.int32, (rows, 128), 1) < HD


def swap(x):
    return pltpu.roll(x, HD, 1)


def pack_kernel(q_ref, k_ref, v_ref, out_ref):
    low_h, low_t = low_lanes(HALF), low_lanes(TOK)
    for pair in range(3):
        lanes = slice(128 * pair, 128 * pair + 128)
        q = q_ref[:, lanes].astype(F32) * 0.125
        k = k_ref[:, lanes].astype(F32)
        v = v_ref[:, lanes].astype(F32)
        top, bottom = q[:HALF], q[HALF:]
        queries = (jnp.where(low_h, top, swap(bottom)), jnp.where(low_h, swap(top), bottom))
        keyvals = (jnp.where(low_t, k, swap(v)), jnp.where(low_t, swap(k), v))
        for side in range(2):
            qh = queries[side].astype(BF)
            kvh = keyvals[side].astype(BF)
            for d in range(NG):
                if HEAD_OF[d] != 2 * pair + side:
                    continue
                size = SIZE_OF[d]
                start = PART_OF[d] * size
                out_ref[d, :HALF, :] = qh
                out_ref[d, HALF : HALF + size, :] = kvh[start : start + size]
                if size < HALF:
                    out_ref[d, HALF + size :, :] = jnp.zeros((HALF - size, 128), BF)


def pieces(x):
    hi = x.astype(BF).astype(F32)
    rest = x - hi
    mid = rest.astype(BF).astype(F32)
    return (hi, mid, rest - mid)


QT = NB * TOK
QP = 2 * QT
KT = NA * NB * HALF
KC = 384
ROWS = 80
KEPT = 48


def attend_kernel(scal_ref, q_ref, kv_ref, out_ref, key_ref, val_ref, query_ref, top_ref, acc_ref):
    first_len, column, size, offset = scal_ref[0], scal_ref[1], scal_ref[2], scal_ref[3]
    row_tok = NA * NB * TOK
    lane3 = lax.broadcasted_iota(jnp.int32, (NA * NB, HALF, 128), 2)
    slot = lax.broadcasted_iota(jnp.int32, (NA * NB, HALF, 128), 1)
    block = lax.broadcasted_iota(jnp.int32, (NA * NB, HALF, 128), 0) * TOK + slot
    low = low_lanes(HALF)
    lane_q = lax.broadcasted_iota(jnp.int32, (16, QT), 1)
    row_q = lax.broadcasted_iota(jnp.int32, (16, QT), 0)
    part = NB * HALF
    ones = (lax.broadcasted_iota(jnp.int32, (ROWS - HD, KC), 0) == 0).astype(F32)
    for j in range(NY):
        pos = jnp.where(slot < size, block + (j * row_tok + offset), LEN_ALL)
        own = jnp.where(pos < first_len, 0, jnp.where(pos < LEN_ALL, 1, -1))
        extra = jnp.where((lane3 < 3) & (lane3 != own), MASKED, 0.0)
        extra = extra.reshape(KT, 128).astype(BF)
        keyvals = jnp.concatenate(
            [kv_ref[(i * NY + j) * part : (i * NY + j + 1) * part, :] for i in range(NA)], axis=0
        )
        turned = keyvals.astype(F32).T
        for i in range(KT // KC):
            rows = slice(i * KC, (i + 1) * KC)
            key_ref[j * (KT // KC) + i, :, :128] = keyvals[rows]
            key_ref[j * (KT // KC) + i, :, 128:] = extra[rows]
            val_ref[j * (KT // KC) + i] = jnp.concatenate(
                [turned[HD:, i * KC : (i + 1) * KC], ones], axis=0
            ).astype(BF)

        stack = []
        for c in range(NB):
            q = q_ref[j * NB + c, :HALF, :].astype(F32)
            stack += [jnp.where(low, q, 0.0), jnp.where(low, swap(q), 0.0)]
        pair, lanes = j // 2, slice(j % 2 * QT, j % 2 * QT + QT)
        query_ref[pair, :128, lanes] = jnp.concatenate(stack, axis=0).T.astype(BF)
        pos = lane_q + (j * row_tok + column * QT)
        own = jnp.where(pos < first_len, 0, jnp.where(pos < LEN_ALL, 1, 2))
        query_ref[pair, 128:144, lanes] = jnp.where(row_q == own, 1.0, 0.0).astype(BF)
        query_ref[pair, 144:, lanes] = jnp.zeros((112, QT), BF)
    top_ref[...] = jnp.full_like(top_ref, FLOOR)
    acc_ref[...] = jnp.zeros_like(acc_ref)

    def holds(start, stop):
        stop = jnp.minimum(stop, LEN_ALL)
        return start < first_len, (stop > first_len) & (start < stop)

    def absorb(j, t, lanes):
        scores = jnp.dot(key_ref[j], query_ref[t, :, lanes], preferred_element_type=F32)
        old = top_ref[t, :1, lanes]
        new = jnp.maximum(jnp.max(scores, axis=0, keepdims=True), old)
        weights = jnp.exp(scores - new).astype(BF)
        acc_ref[t, :, lanes] = acc_ref[t, :, lanes] * jnp.exp(old - new) + jnp.dot(
            val_ref[j], weights, preferred_element_type=F32
        )
        top_ref[t, :, lanes] = jnp.broadcast_to(new, (8, new.shape[1]))

    def visit(number, carry):
        j, t = number // 2, number % 2
        k_first, k_second = holds(j * (2 * KC), (j + 1) * (2 * KC))

        def needed(row):
            start = row * row_tok + column * QT
            q_first, q_second = holds(start, start + QT)
            return (q_first & k_first) | (q_second & k_second)

        left, right = needed(2 * t), needed(2 * t + 1)
        pl.when(left & right)(lambda: absorb(j, t, slice(0, QP)))
        pl.when(left & jnp.logical_not(right))(lambda: absorb(j, t, slice(0, QT)))
        pl.when(right & jnp.logical_not(left))(lambda: absorb(j, t, slice(QT, QP)))
        return carry

    lax.fori_loop(0, NY * KT // KC * 2, visit, 0)

    row8 = lax.broadcasted_iota(jnp.int32, (8, QT), 0)
    lane_m = lax.broadcasted_iota(jnp.int32, (KEPT, 128), 1)
    for t in range(NY):
        pair, lanes = t // 2, slice(t % 2 * QT, t % 2 * QT + QT)
        sums = acc_ref[pair, HD : HD + 1, lanes]
        stats = jnp.zeros((8, QT), F32)
        for number, piece in enumerate(pieces(top_ref[pair, :1, lanes]) + pieces(sums)):
            stats = jnp.where(row8 == number, piece, stats)
        whole = jnp.concatenate(
            [acc_ref[pair, :HD, lanes] * (1.0 / jnp.where(sums > 0.0, sums, 1.0)), stats], axis=0
        )
        for c in range(NB):
            moved = pltpu.roll(whole, QT - c * TOK, 1) if c else whole
            moved = moved[:, :128]
            rest = moved[KEPT:HD]
            thirds = [pltpu.roll(rest, (TOK - 32 * k) % 128, 1) for k in range(3)]
            kept = jnp.where(lane_m < TOK, moved[:KEPT], jnp.concatenate(thirds, axis=0))
            out_ref[t * NB + c] = jnp.concatenate([kept, moved[HD:]], axis=0).astype(BF)


def merge_kernel(part_ref, w_ref, out_ref, att_ref, copy_ref, sem):
    copy = pltpu.make_async_copy(w_ref, copy_ref, sem)
    copy.start()
    lane_r = lax.broadcasted_iota(jnp.int32, (HD - KEPT, 128), 1)
    stat = part_ref[:, KEPT:, :].astype(F32)
    tops = stat[:, 0] + stat[:, 1] + stat[:, 2]
    sums = stat[:, 3] + stat[:, 4] + stat[:, 5]
    for h in range(6):
        own = [d for d in range(NG) if HEAD_OF[d] == h]
        rows = slice(own[0], own[-1] + 1)
        top = jnp.max(tops[rows], axis=0, keepdims=True)
        scaled = jnp.exp(tops[rows] - top) * sums[rows]
        total = jnp.sum(scaled, axis=0, keepdims=True)
        shares = scaled / jnp.where(total > 0.0, total, 1.0)
        mixed = jnp.zeros((HD, 128), F32)
        for i, d in enumerate(own):
            part = part_ref[d, :KEPT, :].astype(F32)
            thirds = [
                pltpu.roll(part[16 * k : 16 * k + 16], (32 * k + 128 - TOK) % 128, 1)
                for k in range(3)
            ]
            rest = jnp.where(
                lane_r < 32, thirds[0], jnp.where(lane_r < 64, thirds[1], thirds[2])
            )
            mixed += shares[i : i + 1] * jnp.concatenate([part, rest], axis=0)
        att_ref[HD * h : HD * h + HD, :] = mixed
    attended = att_ref[...].T[:TOK].astype(BF)
    copy.wait()
    for j in range(NHEAD):
        out_ref[j] = jnp.dot(
            attended, copy_ref[:, 384 * j : 384 * j + 384], preferred_element_type=F32
        ).astype(BF)


def split2(x):
    hi = x.astype(BF)
    return hi, (x - hi.astype(F32)).astype(BF)


def stream_kernel(
    scal_ref, term_ref, hid_ref, gate_ref, shift_ref, scale_ref, w_ref, hid_out, msg_ref
):
    first_len, base = scal_ref[0], scal_ref[4]
    projected = term_ref[0].astype(F32)
    for j in range(1, NHEAD):
        projected += term_ref[j].astype(F32)
    pos = base + lax.broadcasted_iota(jnp.int32, (TOK, 384), 0)
    first, second = pos < first_len, pos < LEN_ALL

    def per_row(table):
        return jnp.where(first, table[0:1], jnp.where(second, table[1:2], 0.0))

    gate, shift = gate_ref[...].astype(F32), shift_ref[...].astype(F32)
    factor = 1.0 + scale_ref[...].astype(F32)
    x = (hid_ref[...].astype(F32) + per_row(gate) * projected).astype(BF)
    hid_out[...] = x
    xf = x.astype(F32)
    own_mean = jnp.sum(xf, axis=1, keepdims=True) * (1.0 / 384)
    scaled = jnp.concatenate(
        [(xf - own_mean) * per_row(factor), factor, shift, jnp.zeros((28, 384), F32)], axis=0
    )
    sq_hi, sq_lo = split2(xf * xf)
    ones = jnp.ones((8, 384), BF)

    def turn(left, right):
        return lax.dot_general(left, right, (((1,), (1,)), ((), ())), preferred_element_type=F32)

    high, rest = split2(scaled)
    w = w_ref[...]
    a = turn(w, high) + turn(w, rest)
    left = pltpu.roll(a - a.astype(BF).astype(F32), 4, 1)
    lane = lax.broadcasted_iota(jnp.int32, (64, 128), 1)
    a = jnp.where((lane >= TOK + 4) & (lane < TOK + 8), left, a).astype(BF)
    total = turn(ones, x)
    squares = turn(ones, sq_hi) + turn(ones, sq_lo)
    rows8 = lax.broadcasted_iota(jnp.int32, (8, TOK), 0)
    tail = jnp.zeros((8, TOK), F32)
    for number, piece in enumerate(pieces(total) + pieces(squares)):
        tail = jnp.where(rows8 == number, piece, tail)
    tail = jnp.concatenate([tail, jnp.zeros((8, 128 - TOK), F32)], axis=1)
    message = jnp.concatenate([a.astype(F32), tail], axis=0).astype(BF)
    for j in range(NHEAD):
        msg_ref[j] = message


def step_kernel(scal_ref, coef_ref, msg_ref, lat_ref, clean_ref, prev_ref):
    first_len, base = scal_ref[0], scal_ref[4]
    pos = base + lax.broadcasted_iota(jnp.int32, (64, TOK), 1)
    first, live = pos < first_len, pos < LEN_ALL
    parts = [msg_ref[j].astype(F32) for j in range(NHEAD)]
    sums = [p[64:65, :TOK] + p[65:66, :TOK] + p[66:67, :TOK] for p in parts]
    squares = [p[67:68, :TOK] + p[68:69, :TOK] + p[69:70, :TOK] for p in parts]
    mean, square = sums[0], squares[0]
    for j in range(1, NHEAD):
        mean, square = mean + sums[j], square + squares[j]
    mean, square = mean * (1.0 / D), square * (1.0 / D)
    var = square - mean * mean
    scaled, shifted = jnp.zeros((64, TOK), F32), jnp.zeros((64, 128), F32)
    for p, own in zip(parts, sums):
        scale_w = jnp.where(
            first,
            p[:64, TOK : TOK + 1] + p[:64, TOK + 4 : TOK + 5],
            p[:64, TOK + 1 : TOK + 2] + p[:64, TOK + 5 : TOK + 6],
        )
        scaled += p[:64, :TOK] + (own * (1.0 / 384) - mean) * scale_w
        shifted += p[:64]
    shift_w = jnp.where(
        first,
        shifted[:, TOK + 2 : TOK + 3] + shifted[:, TOK + 6 : TOK + 7],
        shifted[:, TOK + 3 : TOK + 4] + shifted[:, TOK + 7 : TOK + 8],
    )
    velocity = lax.rsqrt(var + EPSILON) * scaled + shift_w
    latent = lat_ref[...]

    def row_coef(i):
        return jnp.where(first, coef_ref[2 * i], coef_ref[2 * i + 1])

    root_a, root_1a, root_q, root_1q = (row_coef(i) for i in range(4))
    clean = root_a * latent - root_1a * velocity
    noise = root_1a * latent + root_a * velocity
    stepped = root_q * clean + root_1q * noise
    clean_ref[...] = jnp.where(live, clean, 0.0)
    prev_ref[...] = jnp.where(live, stepped, 0.0)


def alpha_table():
    betas = np.linspace(0.00085**0.5, 0.012**0.5, TRAIN_STEPS) ** 2
    return np.cumprod(1.0 - betas).astype(np.float32)


def request_of(position, first_len):
    return jnp.where(
        position < 0, -1, jnp.where(position < first_len, 0, jnp.where(position < LEN_ALL, 1, 2))
    )


def shards(
    lengths,
    step_index,
    query_act,
    key_act,
    value_act,
    hidden,
    attn_weight,
    gate_mod,
    shift_mod,
    scale_mod,
    proj_weight,
    latent,
):
    y, column, c = lax.axis_index("y"), lax.axis_index("a"), lax.axis_index("c")
    seq = (y * NA + column) * NB + c
    member = y * NB + c
    first_len = lengths[0]
    size = jnp.where(member < 12, 32, 48)
    part = jnp.where(member < 12, member % 3, member % 2)
    scal = jnp.stack([first_len, column, size, part * size, seq * TOK]).astype(jnp.int32)
    in_smem = pl.BlockSpec(memory_space=SMEM)
    big = pltpu.CompilerParams(vmem_limit_bytes=48 * 1024 * 1024)
    small = pltpu.CompilerParams(vmem_limit_bytes=8 * 1024 * 1024)

    any_vmem = pl.BlockSpec(memory_space=VMEM)

    packed = pl.pallas_call(
        pack_kernel, out_shape=jax.ShapeDtypeStruct((NG, TOK, 128), BF), name="pack"
    )(query_act, key_act, value_act)
    mine = lax.all_to_all(packed, ("y", "c"), 0, 0, tiled=True)
    keyvals = lax.all_gather(mine[:, HALF:].reshape(NG * HALF, 128), "a", axis=0, tiled=True)
    partial = pl.pallas_call(
        attend_kernel,
        out_shape=jax.ShapeDtypeStruct((NG, KEPT + 8, 128), BF),
        in_specs=[in_smem, any_vmem, any_vmem],
        out_specs=any_vmem,
        scratch_shapes=[
            VMEM((NY * KT // KC, KC, 256), BF),
            VMEM((NY * KT // KC, ROWS, KC), BF),
            VMEM((2, 256, QP), BF),
            VMEM((2, 8, QP), F32),
            VMEM((2, ROWS, QP), F32),
        ],
        compiler_params=big,
        name="attend",
    )(scal, mine, keyvals)
    parts = lax.all_to_all(partial, ("y", "c"), 0, 0, tiled=True)
    term = pl.pallas_call(
        merge_kernel,
        out_shape=jax.ShapeDtypeStruct((NHEAD, TOK, 384), BF),
        in_specs=[any_vmem, pl.BlockSpec(memory_space=pl.ANY)],
        out_specs=any_vmem,
        scratch_shapes=[VMEM((384, 128), F32), VMEM((384, D), BF), pltpu.SemaphoreType.DMA],
        compiler_params=big,
        name="merge",
    )(parts, attn_weight)
    terms = lax.all_to_all(term, ("x", "core"), 0, 0, tiled=True)
    hidden_out, message = pl.pallas_call(
        stream_kernel,
        out_shape=(
            jax.ShapeDtypeStruct((TOK, 384), BF),
            jax.ShapeDtypeStruct((NHEAD, 72, 128), BF),
        ),
        in_specs=[in_smem] + [any_vmem] * 6,
        compiler_params=small,
        name="stream",
    )(scal, terms, hidden, gate_mod, shift_mod, scale_mod, proj_weight.T)
    message = lax.all_to_all(message, ("x", "core"), 0, 0, tiled=True)
    table = jnp.asarray(alpha_table())
    alpha_now = table[step_index]
    alpha_prev = table[step_index - STEP_GAP]
    coef = jnp.concatenate(
        [
            jnp.sqrt(alpha_now),
            jnp.sqrt(1.0 - alpha_now),
            jnp.sqrt(alpha_prev),
            jnp.sqrt(1.0 - alpha_prev),
        ]
    )
    clean, stepped = pl.pallas_call(
        step_kernel,
        out_shape=(jax.ShapeDtypeStruct((64, TOK), F32),) * 2,
        in_specs=[in_smem, in_smem, any_vmem, any_vmem],
        compiler_params=small,
        name="ddim",
    )(scal, coef, message, latent.T)
    pairs = []
    for s in range(NY * NA * NB):
        for x in range(NX):
            up, down = (s * NX + x) * NC, (s * NX + x) * NC + 1
            if s + 1 < NY * NA * NB:
                pairs.append((up, up + NX * NC))
            if s > 0:
                pairs.append((down, down - NX * NC))
    got = lax.ppermute(stepped, ("y", "a", "c", "x", "core"), pairs)
    both = lax.all_gather(got, "core")
    offsets = jnp.arange(RIM, dtype=jnp.int32)
    start = seq * TOK
    lower_ok = request_of(start - RIM + offsets, first_len) == request_of(start, first_len)
    upper_ok = request_of(start + TOK + offsets, first_len) == request_of(
        start + TOK - 1, first_len
    )
    lower_ok &= start > 0
    upper_ok &= start + TOK < NY * NA * NB * TOK
    rims = jnp.concatenate(
        [
            jnp.where(lower_ok[None], both[0, :, TOK - RIM :], 0.0),
            jnp.where(upper_ok[None], both[1, :, :RIM], 0.0),
        ],
        axis=1,
    )
    return hidden_out, clean.T, stepped.T, rims.T


def solution(mesh):
    grid = Mesh(mesh.devices.reshape(NY, NA, NB, NX, NC), ("y", "a", "c", "x", "core"))
    seq, head = ("y", "a", "c"), ("x", "core")
    in_specs = (
        P(),
        P(),
        P(seq, head),
        P(seq, head),
        P(seq, head),
        P(seq, head),
        P(head, None),
        P(None, head),
        P(None, head),
        P(None, head),
        P(head, None),
        P(seq, None),
    )
    out_specs = (P(seq, head), P(seq, None), P(seq, None), P(seq, None))
    return jax.shard_map(shards, mesh=grid, in_specs=in_specs, out_specs=out_specs, check_vma=False)
```

```python
import jax
import jax.numpy as jnp
import numpy as np
from jax import lax
from jax.experimental import pallas as pl
from jax.experimental.pallas import tpu as pltpu
from jax.sharding import Mesh
from jax.sharding import PartitionSpec as P

D = 3072
HD = 64
RIM = 45
TOK = 96
HALF = 48
LEN_ALL = 5952
TRAIN_STEPS = 1000
STEP_GAP = 20
NY, NA, NB, NX, NC = 4, 4, 4, 4, 2
NG = NY * NB
NHEAD = 8
EPSILON = 1e-06
MASKED = -1e30
FLOOR = -0.5e30
HEAD_OF = (0, 0, 0, 1, 1, 1, 2, 2, 2, 3, 3, 3, 4, 4, 5, 5)
PART_OF = (0, 1, 2, 0, 1, 2, 0, 1, 2, 0, 1, 2, 0, 1, 0, 1)
SIZE_OF = (32,) * 12 + (48,) * 4
BF = jnp.bfloat16
F32 = jnp.float32
SMEM = pltpu.SMEM
VMEM = pltpu.VMEM


def low_lanes(rows):
    return lax.broadcasted_iota(jnp.int32, (rows, 128), 1) < HD


def swap(x):
    return pltpu.roll(x, HD, 1)


def pack_kernel(q_ref, k_ref, v_ref, out_ref):
    low_h, low_t = low_lanes(HALF), low_lanes(TOK)
    for pair in range(3):
        lanes = slice(128 * pair, 128 * pair + 128)
        q = q_ref[:, lanes].astype(F32) * 0.125
        k = k_ref[:, lanes].astype(F32)
        v = v_ref[:, lanes].astype(F32)
        top, bottom = q[:HALF], q[HALF:]
        queries = (jnp.where(low_h, top, swap(bottom)), jnp.where(low_h, swap(top), bottom))
        keyvals = (jnp.where(low_t, k, swap(v)), jnp.where(low_t, swap(k), v))
        for side in range(2):
            qh = queries[side].astype(BF)
            kvh = keyvals[side].astype(BF)
            for d in range(NG):
                if HEAD_OF[d] != 2 * pair + side:
                    continue
                size = SIZE_OF[d]
                start = PART_OF[d] * size
                out_ref[d, :HALF, :] = qh
                out_ref[d, HALF : HALF + size, :] = kvh[start : start + size]
                if size < HALF:
                    out_ref[d, HALF + size :, :] = jnp.zeros((HALF - size, 128), BF)


def pieces(x):
    hi = x.astype(BF).astype(F32)
    rest = x - hi
    mid = rest.astype(BF).astype(F32)
    return (hi, mid, rest - mid)


QT = NB * TOK
QP = 2 * QT
KT = NA * NB * HALF
KC = 768
ROWS = 80
KEPT = 48


def attend_kernel(scal_ref, q_ref, kv_ref, out_ref, key_ref, val_ref, query_ref, top_ref, acc_ref):
    first_len, column, size, offset = scal_ref[0], scal_ref[1], scal_ref[2], scal_ref[3]
    row_tok = NA * NB * TOK
    lane3 = lax.broadcasted_iota(jnp.int32, (NA * NB, HALF, 128), 2)
    slot = lax.broadcasted_iota(jnp.int32, (NA * NB, HALF, 128), 1)
    block = lax.broadcasted_iota(jnp.int32, (NA * NB, HALF, 128), 0) * TOK + slot + offset
    block = jnp.where(slot < size, block, NY * row_tok)
    low = low_lanes(HALF)
    lane_q = lax.broadcasted_iota(jnp.int32, (16, QT), 1)
    row_q = lax.broadcasted_iota(jnp.int32, (16, QT), 0)
    part = NB * HALF
    ones = (lax.broadcasted_iota(jnp.int32, (ROWS - HD, KC), 0) == 0).astype(F32)
    for j in range(NY):
        own = jnp.where(block < first_len - j * row_tok, 0, jnp.where(block < LEN_ALL - j * row_tok, 1, 2))
        extra = jnp.where(lane3 == own, 1.0, 0.0)
        extra = extra.reshape(KT, 128).astype(BF)
        keyvals = jnp.concatenate(
            [kv_ref[(i * NY + j) * part : (i * NY + j + 1) * part, :] for i in range(NA)], axis=0
        )
        turned = keyvals.astype(F32).T
        for i in range(KT // KC):
            rows = slice(i * KC, (i + 1) * KC)
            key_ref[j * (KT // KC) + i, :, :128] = keyvals[rows]
            key_ref[j * (KT // KC) + i, :, 128:] = extra[rows]
            val_ref[j * (KT // KC) + i] = jnp.concatenate(
                [turned[HD:, i * KC : (i + 1) * KC], ones], axis=0
            ).astype(BF)

        stack = []
        for c in range(NB):
            q = q_ref[j * NB + c, :HALF, :].astype(F32)
            stack += [jnp.where(low, q, 0.0), jnp.where(low, swap(q), 0.0)]
        pair, lanes = j // 2, slice(j % 2 * QT, j % 2 * QT + QT)
        query_ref[pair, :128, lanes] = jnp.concatenate(stack, axis=0).T.astype(BF)
        pos = lane_q + (j * row_tok + column * QT)
        own = jnp.where(pos < first_len, 0, jnp.where(pos < LEN_ALL, 1, 2))
        query_ref[pair, 128:144, lanes] = jnp.where((row_q < 3) & ((row_q != own) | (own == 2)), MASKED, 0.0).astype(BF)
        query_ref[pair, 144:, lanes] = jnp.zeros((112, QT), BF)
    top_ref[...] = jnp.full_like(top_ref, FLOOR)
    acc_ref[...] = jnp.zeros_like(acc_ref)

    def holds(start, stop):
        stop = jnp.minimum(stop, LEN_ALL)
        return start < first_len, (stop > first_len) & (start < stop)

    def absorb(j, t, lanes):
        scores = jnp.dot(key_ref[j], query_ref[t, :, lanes], preferred_element_type=F32)
        old = top_ref[t, :1, lanes]
        new = jnp.maximum(jnp.max(scores, axis=0, keepdims=True), old)
        weights = jnp.exp(scores - new).astype(BF)
        acc_ref[t, :, lanes] = acc_ref[t, :, lanes] * jnp.exp(old - new) + jnp.dot(
            val_ref[j], weights, preferred_element_type=F32
        )
        top_ref[t, :, lanes] = jnp.broadcast_to(new, (8, new.shape[1]))

    def visit(number, carry):
        j, t = number // 2, number % 2
        k_first, k_second = holds(j * (2 * KC), (j + 1) * (2 * KC))

        def needed(row):
            start = row * row_tok + column * QT
            q_first, q_second = holds(start, start + QT)
            return (q_first & k_first) | (q_second & k_second)

        left, right = needed(2 * t), needed(2 * t + 1)
        pl.when(left & right)(lambda: absorb(j, t, slice(0, QP)))
        pl.when(left & jnp.logical_not(right))(lambda: absorb(j, t, slice(0, QT)))
        pl.when(right & jnp.logical_not(left))(lambda: absorb(j, t, slice(QT, QP)))
        return carry

    lax.fori_loop(0, NY * KT // KC * 2, visit, 0)

    row8 = lax.broadcasted_iota(jnp.int32, (8, QT), 0)
    lane_m = lax.broadcasted_iota(jnp.int32, (KEPT, 128), 1)
    for t in range(NY):
        pair, lanes = t // 2, slice(t % 2 * QT, t % 2 * QT + QT)
        sums = acc_ref[pair, HD : HD + 1, lanes]
        stats = jnp.zeros((8, QT), F32)
        for number, piece in enumerate(pieces(top_ref[pair, :1, lanes]) + pieces(sums)):
            stats = jnp.where(row8 == number, piece, stats)
        whole = jnp.concatenate(
            [acc_ref[pair, :HD, lanes] * (1.0 / jnp.where(sums > 0.0, sums, 1.0)), stats], axis=0
        )
        for c in range(NB):
            moved = pltpu.roll(whole, QT - c * TOK, 1) if c else whole
            moved = moved[:, :128]
            rest = moved[KEPT:HD]
            thirds = [pltpu.roll(rest, (TOK - 32 * k) % 128, 1) for k in range(3)]
            kept = jnp.where(lane_m < TOK, moved[:KEPT], jnp.concatenate(thirds, axis=0))
            out_ref[t * NB + c] = jnp.concatenate([kept, moved[HD:]], axis=0).astype(BF)


def merge_kernel(part_ref, w_ref, out_ref, att_ref, copy_ref, sem):
    copy = pltpu.make_async_copy(w_ref, copy_ref, sem)
    copy.start()
    lane_r = lax.broadcasted_iota(jnp.int32, (HD - KEPT, 128), 1)
    stat = part_ref[:, KEPT:, :].astype(F32)
    tops = stat[:, 0] + stat[:, 1] + stat[:, 2]
    sums = stat[:, 3] + stat[:, 4] + stat[:, 5]
    for h in range(6):
        own = [d for d in range(NG) if HEAD_OF[d] == h]
        rows = slice(own[0], own[-1] + 1)
        top = jnp.max(tops[rows], axis=0, keepdims=True)
        scaled = jnp.exp(tops[rows] - top) * sums[rows]
        total = jnp.sum(scaled, axis=0, keepdims=True)
        shares = scaled / jnp.where(total > 0.0, total, 1.0)
        mixed = jnp.zeros((HD, 128), F32)
        for i, d in enumerate(own):
            part = part_ref[d, :KEPT, :].astype(F32)
            thirds = [
                pltpu.roll(part[16 * k : 16 * k + 16], (32 * k + 128 - TOK) % 128, 1)
                for k in range(3)
            ]
            rest = jnp.where(
                lane_r < 32, thirds[0], jnp.where(lane_r < 64, thirds[1], thirds[2])
            )
            mixed += shares[i : i + 1] * jnp.concatenate([part, rest], axis=0)
        att_ref[HD * h : HD * h + HD, :] = mixed
    attended = att_ref[...].T[:TOK].astype(BF)
    copy.wait()
    for j in range(NHEAD):
        out_ref[j] = jnp.dot(
            attended, copy_ref[:, 384 * j : 384 * j + 384], preferred_element_type=F32
        ).astype(BF)


def split2(x):
    hi = x.astype(BF)
    return hi, (x - hi.astype(F32)).astype(BF)


def stream_kernel(
    scal_ref, term_ref, hid_ref, gate_ref, shift_ref, scale_ref, w_ref, hid_out, msg_ref
):
    first_len, base = scal_ref[0], scal_ref[4]
    projected = term_ref[0].astype(F32)
    for j in range(1, NHEAD):
        projected += term_ref[j].astype(F32)
    pos = base + lax.broadcasted_iota(jnp.int32, (TOK, 384), 0)
    first, second = pos < first_len, pos < LEN_ALL

    def per_row(table):
        return jnp.where(first, table[0:1], jnp.where(second, table[1:2], 0.0))

    gate, shift = gate_ref[...].astype(F32), shift_ref[...].astype(F32)
    factor = 1.0 + scale_ref[...].astype(F32)
    x = (hid_ref[...].astype(F32) + per_row(gate) * projected).astype(BF)
    hid_out[...] = x
    xf = x.astype(F32)
    own_mean = jnp.sum(xf, axis=1, keepdims=True) * (1.0 / 384)
    scaled = jnp.concatenate(
        [(xf - own_mean) * per_row(factor), factor, shift, jnp.zeros((28, 384), F32)], axis=0
    )
    sq_hi, sq_lo = split2(xf * xf)
    ones = jnp.ones((8, 384), BF)

    def turn(left, right):
        return lax.dot_general(left, right, (((1,), (1,)), ((), ())), preferred_element_type=F32)

    high, rest = split2(scaled)
    w = w_ref[...]
    a = turn(w, high) + turn(w, rest)
    left = pltpu.roll(a - a.astype(BF).astype(F32), 4, 1)
    lane = lax.broadcasted_iota(jnp.int32, (64, 128), 1)
    a = jnp.where((lane >= TOK + 4) & (lane < TOK + 8), left, a).astype(BF)
    total = turn(ones, x)
    squares = turn(ones, sq_hi) + turn(ones, sq_lo)
    rows8 = lax.broadcasted_iota(jnp.int32, (8, TOK), 0)
    tail = jnp.zeros((8, TOK), F32)
    for number, piece in enumerate(pieces(total) + pieces(squares)):
        tail = jnp.where(rows8 == number, piece, tail)
    tail = jnp.concatenate([tail, jnp.zeros((8, 128 - TOK), F32)], axis=1)
    message = jnp.concatenate([a.astype(F32), tail], axis=0).astype(BF)
    for j in range(NHEAD):
        msg_ref[j] = message


def step_kernel(scal_ref, coef_ref, msg_ref, lat_ref, clean_ref, prev_ref):
    first_len, base = scal_ref[0], scal_ref[4]
    pos = base + lax.broadcasted_iota(jnp.int32, (64, TOK), 1)
    first, live = pos < first_len, pos < LEN_ALL
    parts = [msg_ref[j].astype(F32) for j in range(NHEAD)]
    sums = [p[64:65, :TOK] + p[65:66, :TOK] + p[66:67, :TOK] for p in parts]
    squares = [p[67:68, :TOK] + p[68:69, :TOK] + p[69:70, :TOK] for p in parts]
    mean, square = sums[0], squares[0]
    for j in range(1, NHEAD):
        mean, square = mean + sums[j], square + squares[j]
    mean, square = mean * (1.0 / D), square * (1.0 / D)
    var = square - mean * mean
    scaled, shifted = jnp.zeros((64, TOK), F32), jnp.zeros((64, 128), F32)
    for p, own in zip(parts, sums):
        scale_w = jnp.where(
            first,
            p[:64, TOK : TOK + 1] + p[:64, TOK + 4 : TOK + 5],
            p[:64, TOK + 1 : TOK + 2] + p[:64, TOK + 5 : TOK + 6],
        )
        scaled += p[:64, :TOK] + (own * (1.0 / 384) - mean) * scale_w
        shifted += p[:64]
    shift_w = jnp.where(
        first,
        shifted[:, TOK + 2 : TOK + 3] + shifted[:, TOK + 6 : TOK + 7],
        shifted[:, TOK + 3 : TOK + 4] + shifted[:, TOK + 7 : TOK + 8],
    )
    velocity = lax.rsqrt(var + EPSILON) * scaled + shift_w
    latent = lat_ref[...]

    def row_coef(i):
        return jnp.where(first, coef_ref[2 * i], coef_ref[2 * i + 1])

    root_a, root_1a, root_q, root_1q = (row_coef(i) for i in range(4))
    clean = root_a * latent - root_1a * velocity
    noise = root_1a * latent + root_a * velocity
    stepped = root_q * clean + root_1q * noise
    clean_ref[...] = jnp.where(live, clean, 0.0)
    prev_ref[...] = jnp.where(live, stepped, 0.0)


def alpha_table():
    betas = np.linspace(0.00085**0.5, 0.012**0.5, TRAIN_STEPS) ** 2
    return np.cumprod(1.0 - betas).astype(np.float32)


def request_of(position, first_len):
    return jnp.where(
        position < 0, -1, jnp.where(position < first_len, 0, jnp.where(position < LEN_ALL, 1, 2))
    )


def shards(
    lengths,
    step_index,
    query_act,
    key_act,
    value_act,
    hidden,
    attn_weight,
    gate_mod,
    shift_mod,
    scale_mod,
    proj_weight,
    latent,
):
    y, column, c = lax.axis_index("y"), lax.axis_index("a"), lax.axis_index("c")
    seq = (y * NA + column) * NB + c
    member = y * NB + c
    first_len = lengths[0]
    size = jnp.where(member < 12, 32, 48)
    part = jnp.where(member < 12, member % 3, member % 2)
    scal = jnp.stack([first_len, column, size, part * size, seq * TOK]).astype(jnp.int32)
    in_smem = pl.BlockSpec(memory_space=SMEM)
    big = pltpu.CompilerParams(vmem_limit_bytes=24 * 1024 * 1024)
    small = pltpu.CompilerParams(vmem_limit_bytes=8 * 1024 * 1024)

    any_vmem = pl.BlockSpec(memory_space=VMEM)

    packed = pl.pallas_call(
        pack_kernel, out_shape=jax.ShapeDtypeStruct((NG, TOK, 128), BF), name="pack"
    )(query_act, key_act, value_act)
    mine = lax.all_to_all(packed, ("y", "c"), 0, 0, tiled=True)
    keyvals = lax.all_gather(mine[:, HALF:].reshape(NG * HALF, 128), "a", axis=0, tiled=True)
    partial = pl.pallas_call(
        attend_kernel,
        out_shape=jax.ShapeDtypeStruct((NG, KEPT + 8, 128), BF),
        in_specs=[in_smem, any_vmem, any_vmem],
        out_specs=any_vmem,
        scratch_shapes=[
            VMEM((NY * KT // KC, KC, 256), BF),
            VMEM((NY * KT // KC, ROWS, KC), BF),
            VMEM((2, 256, QP), BF),
            VMEM((2, 8, QP), F32),
            VMEM((2, ROWS, QP), F32),
        ],
        compiler_params=big,
        name="attend",
    )(scal, mine, keyvals)
    parts = lax.all_to_all(partial, ("y", "c"), 0, 0, tiled=True)
    term = pl.pallas_call(
        merge_kernel,
        out_shape=jax.ShapeDtypeStruct((NHEAD, TOK, 384), BF),
        in_specs=[any_vmem, pl.BlockSpec(memory_space=pl.ANY)],
        out_specs=any_vmem,
        scratch_shapes=[VMEM((384, 128), F32), VMEM((384, D), BF), pltpu.SemaphoreType.DMA],
        compiler_params=big,
        name="merge",
    )(parts, attn_weight)
    terms = lax.all_to_all(term, ("x", "core"), 0, 0, tiled=True)
    hidden_out, message = pl.pallas_call(
        stream_kernel,
        out_shape=(
            jax.ShapeDtypeStruct((TOK, 384), BF),
            jax.ShapeDtypeStruct((NHEAD, 72, 128), BF),
        ),
        in_specs=[in_smem] + [any_vmem] * 6,
        compiler_params=small,
        name="stream",
    )(scal, terms, hidden, gate_mod, shift_mod, scale_mod, proj_weight.T)
    message = lax.all_to_all(message, ("x", "core"), 0, 0, tiled=True)
    table = jnp.asarray(alpha_table())
    alpha_now = table[step_index]
    alpha_prev = table[step_index - STEP_GAP]
    coef = jnp.concatenate(
        [
            jnp.sqrt(alpha_now),
            jnp.sqrt(1.0 - alpha_now),
            jnp.sqrt(alpha_prev),
            jnp.sqrt(1.0 - alpha_prev),
        ]
    )
    clean, stepped = pl.pallas_call(
        step_kernel,
        out_shape=(jax.ShapeDtypeStruct((64, TOK), F32),) * 2,
        in_specs=[in_smem, in_smem, any_vmem, any_vmem],
        compiler_params=small,
        name="ddim",
    )(scal, coef, message, latent.T)
    pairs = []
    for s in range(NY * NA * NB):
        for x in range(NX):
            up, down = (s * NX + x) * NC, (s * NX + x) * NC + 1
            if s + 1 < NY * NA * NB:
                pairs.append((up, up + NX * NC))
            if s > 0:
                pairs.append((down, down - NX * NC))
    got = lax.ppermute(stepped, ("y", "a", "c", "x", "core"), pairs)
    both = lax.all_gather(got, "core")
    offsets = jnp.arange(RIM, dtype=jnp.int32)
    start = seq * TOK
    lower_ok = request_of(start - RIM + offsets, first_len) == request_of(start, first_len)
    upper_ok = request_of(start + TOK + offsets, first_len) == request_of(
        start + TOK - 1, first_len
    )
    lower_ok &= start > 0
    upper_ok &= start + TOK < NY * NA * NB * TOK
    rims = jnp.concatenate(
        [
            jnp.where(lower_ok[None], both[0, :, TOK - RIM :], 0.0),
            jnp.where(upper_ok[None], both[1, :, :RIM], 0.0),
        ],
        axis=1,
    )
    return hidden_out, clean.T, stepped.T, rims.T


def solution(mesh):
    grid = Mesh(mesh.devices.reshape(NY, NA, NB, NX, NC), ("y", "a", "c", "x", "core"))
    seq, head = ("y", "a", "c"), ("x", "core")
    in_specs = (
        P(),
        P(),
        P(seq, head),
        P(seq, head),
        P(seq, head),
        P(seq, head),
        P(head, None),
        P(None, head),
        P(None, head),
        P(None, head),
        P(head, None),
        P(seq, None),
    )
    out_specs = (P(seq, head), P(seq, None), P(seq, None), P(seq, None))
    return jax.shard_map(shards, mesh=grid, in_specs=in_specs, out_specs=out_specs, check_vma=False)
```

```python
import jax
import jax.numpy as jnp
import numpy as np
from jax import lax
from jax.experimental import pallas as pl
from jax.experimental.pallas import tpu as pltpu
from jax.sharding import Mesh
from jax.sharding import PartitionSpec as P

D = 3072
HD = 64
RIM = 45
TOK = 96
HALF = 48
LEN_ALL = 5952
TRAIN_STEPS = 1000
STEP_GAP = 20
NY, NA, NB, NX, NC = 4, 4, 4, 4, 2
NG = NA * NB
NHEAD = 8
EPSILON = 1e-06
MASKED = -1e30
FLOOR = -0.5e30
HEAD_OF = (0, 0, 0, 1, 1, 1, 2, 2, 2, 3, 3, 3, 4, 4, 5, 5)
PART_OF = (0, 1, 2, 0, 1, 2, 0, 1, 2, 0, 1, 2, 0, 1, 0, 1)
SIZE_OF = (32,) * 12 + (48,) * 4
BF = jnp.bfloat16
F32 = jnp.float32
SMEM = pltpu.SMEM
VMEM = pltpu.VMEM


def low_lanes(rows):
    return lax.broadcasted_iota(jnp.int32, (rows, 128), 1) < HD


def swap(x):
    return pltpu.roll(x, HD, 1)


def pack_kernel(q_ref, k_ref, v_ref, out_ref):
    low_h, low_t = low_lanes(HALF), low_lanes(TOK)
    for pair in range(3):
        lanes = slice(128 * pair, 128 * pair + 128)
        q = q_ref[:, lanes].astype(F32) * 0.125
        k = k_ref[:, lanes].astype(F32)
        v = v_ref[:, lanes].astype(F32)
        top, bottom = q[:HALF], q[HALF:]
        queries = (jnp.where(low_h, top, swap(bottom)), jnp.where(low_h, swap(top), bottom))
        keyvals = (jnp.where(low_t, k, swap(v)), jnp.where(low_t, swap(k), v))
        for side in range(2):
            qh = queries[side].astype(BF)
            kvh = keyvals[side].astype(BF)
            for d in range(NG):
                if HEAD_OF[d] != 2 * pair + side:
                    continue
                size = SIZE_OF[d]
                start = PART_OF[d] * size
                out_ref[d, :HALF, :] = qh
                out_ref[d, HALF : HALF + size, :] = kvh[start : start + size]
                if size < HALF:
                    out_ref[d, HALF + size :, :] = jnp.zeros((HALF - size, 128), BF)


def pieces(x):
    hi = x.astype(BF).astype(F32)
    rest = x - hi
    mid = rest.astype(BF).astype(F32)
    return (hi, mid, rest - mid)


QT = NB * TOK
QP = 2 * QT
KT = NA * NB * HALF
KC = KT // 2
ROWS = 80
KEPT = 48


def attend_kernel(scal_ref, q_ref, kv_ref, out_ref, key_ref, val_ref, query_ref, top_ref, acc_ref):
    first_len, row, size, offset = scal_ref[0], scal_ref[1], scal_ref[2], scal_ref[3]
    row_tok = NA * NB * TOK
    lane3 = lax.broadcasted_iota(jnp.int32, (NA * NB, HALF, 128), 2)
    slot = lax.broadcasted_iota(jnp.int32, (NA * NB, HALF, 128), 1)
    block = lax.broadcasted_iota(jnp.int32, (NA * NB, HALF, 128), 0) * TOK + slot + offset
    block = jnp.where(slot < size, block, NY * row_tok)
    low = low_lanes(HALF)
    lane_q = lax.broadcasted_iota(jnp.int32, (16, QT), 1)
    row_q = lax.broadcasted_iota(jnp.int32, (16, QT), 0)
    ones = (lax.broadcasted_iota(jnp.int32, (ROWS - HD, KT), 0) == 0).astype(F32)
    for j in range(NY):
        own = jnp.where(block < first_len - j * row_tok, 0, jnp.where(block < LEN_ALL - j * row_tok, 1, 2))
        extra = jnp.where(lane3 == own, 1.0, 0.0)
        extra = extra.reshape(KT, 128).astype(BF)
        keyvals = kv_ref[j * KT : (j + 1) * KT, :]
        turned = keyvals.astype(F32).T
        key_ref[j * KT : (j + 1) * KT, :128] = keyvals
        key_ref[j * KT : (j + 1) * KT, 128:] = extra
        val_ref[j] = jnp.concatenate([turned[HD:], ones], axis=0).astype(BF)

        stack = []
        for c in range(NB):
            q = q_ref[j * NB + c, :HALF, :].astype(F32)
            stack += [jnp.where(low, q, 0.0), jnp.where(low, swap(q), 0.0)]
        pair, lanes = j // 2, slice(j % 2 * QT, j % 2 * QT + QT)
        query_ref[pair, :128, lanes] = jnp.concatenate(stack, axis=0).T.astype(BF)
        pos = lane_q + (row * row_tok + j * QT)
        own = jnp.where(pos < first_len, 0, jnp.where(pos < LEN_ALL, 1, 2))
        query_ref[pair, 128:144, lanes] = jnp.where((row_q < 3) & ((row_q != own) | (own == 2)), MASKED, 0.0).astype(BF)
        query_ref[pair, 144:, lanes] = jnp.zeros((112, QT), BF)
    top_ref[...] = jnp.full_like(top_ref, FLOOR)
    acc_ref[...] = jnp.zeros_like(acc_ref)

    def holds(start, stop):
        stop = jnp.minimum(stop, LEN_ALL)
        return start < first_len, (stop > first_len) & (start < stop)

    def absorb(keys, values, t, lanes):
        scores = jnp.dot(keys, query_ref[t, :, lanes], preferred_element_type=F32)
        old = top_ref[t, :1, lanes]
        new = jnp.maximum(jnp.max(scores, axis=0, keepdims=True), old)
        weights = jnp.exp(scores - new).astype(BF)
        acc_ref[t, :, lanes] = acc_ref[t, :, lanes] * jnp.exp(old - new) + jnp.dot(
            values, weights, preferred_element_type=F32
        )
        top_ref[t, :, lanes] = jnp.broadcast_to(new, (8, new.shape[1]))

    def visit(number, carry):
        j, t = number // 2, number % 2

        def needed(half, side):
            start = row * row_tok + (2 * t + side) * QT
            q_first, q_second = holds(start, start + QT)
            begin = j * row_tok + half * (row_tok // 2)
            k_first, k_second = holds(begin, begin + row_tok // 2)
            return (q_first & k_first) | (q_second & k_second)

        need = [[needed(half, side) for side in range(2)] for half in range(2)]
        every = need[0][0] & need[0][1] & need[1][0] & need[1][1]

        @pl.when(every)
        def _():
            rows = pl.ds(pl.multiple_of(j * KT, KT), KT)
            absorb(key_ref[rows, :], val_ref[j], t, slice(0, QP))

        @pl.when(jnp.logical_not(every))
        def _():
            for half in range(2):
                left, right = need[half]

                def take(lanes):
                    rows = pl.ds(pl.multiple_of(j * KT + half * KC, KC), KC)
                    values = val_ref[j, :, half * KC : (half + 1) * KC]
                    absorb(key_ref[rows, :], values, t, lanes)

                pl.when(left & right)(lambda: take(slice(0, QP)))
                pl.when(left & jnp.logical_not(right))(lambda: take(slice(0, QT)))
                pl.when(right & jnp.logical_not(left))(lambda: take(slice(QT, QP)))

        return carry

    lax.fori_loop(0, NY * 2, visit, 0)

    row8 = lax.broadcasted_iota(jnp.int32, (8, QT), 0)
    lane_m = lax.broadcasted_iota(jnp.int32, (KEPT, 128), 1)
    for t in range(NY):
        pair, lanes = t // 2, slice(t % 2 * QT, t % 2 * QT + QT)
        sums = acc_ref[pair, HD : HD + 1, lanes]
        stats = jnp.zeros((8, QT), F32)
        for number, piece in enumerate(pieces(top_ref[pair, :1, lanes]) + pieces(sums)):
            stats = jnp.where(row8 == number, piece, stats)
        whole = jnp.concatenate(
            [acc_ref[pair, :HD, lanes] * (1.0 / jnp.where(sums > 0.0, sums, 1.0)), stats], axis=0
        )
        for c in range(NB):
            moved = pltpu.roll(whole, QT - c * TOK, 1) if c else whole
            moved = moved[:, :128]
            rest = moved[KEPT:HD]
            thirds = [pltpu.roll(rest, (TOK - 32 * k) % 128, 1) for k in range(3)]
            kept = jnp.where(lane_m < TOK, moved[:KEPT], jnp.concatenate(thirds, axis=0))
            out_ref[t * NB + c] = jnp.concatenate([kept, moved[HD:]], axis=0).astype(BF)


def merge_kernel(part_ref, w_ref, out_ref, att_ref, copy_ref, sem):
    copy = pltpu.make_async_copy(w_ref, copy_ref, sem)
    copy.start()
    lane_r = lax.broadcasted_iota(jnp.int32, (HD - KEPT, 128), 1)
    stat = part_ref[:, KEPT:, :].astype(F32)
    tops = stat[:, 0] + stat[:, 1] + stat[:, 2]
    sums = stat[:, 3] + stat[:, 4] + stat[:, 5]
    for h in range(6):
        own = [d for d in range(NG) if HEAD_OF[d] == h]
        rows = slice(own[0], own[-1] + 1)
        top = jnp.max(tops[rows], axis=0, keepdims=True)
        scaled = jnp.exp(tops[rows] - top) * sums[rows]
        total = jnp.sum(scaled, axis=0, keepdims=True)
        shares = scaled / jnp.where(total > 0.0, total, 1.0)
        mixed = jnp.zeros((HD, 128), F32)
        for i, d in enumerate(own):
            part = part_ref[d, :KEPT, :].astype(F32)
            thirds = [
                pltpu.roll(part[16 * k : 16 * k + 16], (32 * k + 128 - TOK) % 128, 1)
                for k in range(3)
            ]
            rest = jnp.where(
                lane_r < 32, thirds[0], jnp.where(lane_r < 64, thirds[1], thirds[2])
            )
            mixed += shares[i : i + 1] * jnp.concatenate([part, rest], axis=0)
        att_ref[HD * h : HD * h + HD, :] = mixed
    attended = att_ref[...].T[:TOK].astype(BF)
    copy.wait()
    for j in range(NHEAD):
        out_ref[j] = jnp.dot(
            attended, copy_ref[:, 384 * j : 384 * j + 384], preferred_element_type=F32
        ).astype(BF)


def split2(x):
    hi = x.astype(BF)
    return hi, (x - hi.astype(F32)).astype(BF)


def stream_kernel(
    scal_ref, term_ref, hid_ref, gate_ref, shift_ref, scale_ref, w_ref, hid_out, msg_ref
):
    first_len, base = scal_ref[0], scal_ref[4]
    projected = term_ref[0].astype(F32)
    for j in range(1, NHEAD):
        projected += term_ref[j].astype(F32)
    pos = base + lax.broadcasted_iota(jnp.int32, (TOK, 384), 0)
    first, second = pos < first_len, pos < LEN_ALL

    def per_row(table):
        return jnp.where(first, table[0:1], jnp.where(second, table[1:2], 0.0))

    gate, shift = gate_ref[...].astype(F32), shift_ref[...].astype(F32)
    factor = 1.0 + scale_ref[...].astype(F32)
    x = (hid_ref[...].astype(F32) + per_row(gate) * projected).astype(BF)
    hid_out[...] = x
    xf = x.astype(F32)
    own_mean = jnp.sum(xf, axis=1, keepdims=True) * (1.0 / 384)
    scaled = jnp.concatenate(
        [(xf - own_mean) * per_row(factor), factor, shift, jnp.zeros((28, 384), F32)], axis=0
    )
    sq_hi, sq_lo = split2(xf * xf)
    ones = jnp.ones((8, 384), BF)

    def turn(left, right):
        return lax.dot_general(left, right, (((1,), (1,)), ((), ())), preferred_element_type=F32)

    high, rest = split2(scaled)
    w = w_ref[...]
    a = turn(w, high) + turn(w, rest)
    left = pltpu.roll(a - a.astype(BF).astype(F32), 4, 1)
    lane = lax.broadcasted_iota(jnp.int32, (64, 128), 1)
    a = jnp.where((lane >= TOK + 4) & (lane < TOK + 8), left, a).astype(BF)
    total = turn(ones, x)
    squares = turn(ones, sq_hi) + turn(ones, sq_lo)
    rows8 = lax.broadcasted_iota(jnp.int32, (8, TOK), 0)
    tail = jnp.zeros((8, TOK), F32)
    for number, piece in enumerate(pieces(total) + pieces(squares)):
        tail = jnp.where(rows8 == number, piece, tail)
    tail = jnp.concatenate([tail, jnp.zeros((8, 128 - TOK), F32)], axis=1)
    message = jnp.concatenate([a.astype(F32), tail], axis=0).astype(BF)
    for j in range(NHEAD):
        msg_ref[j] = message


def step_kernel(scal_ref, coef_ref, msg_ref, lat_ref, clean_ref, prev_ref):
    first_len, base = scal_ref[0], scal_ref[4]
    pos = base + lax.broadcasted_iota(jnp.int32, (64, TOK), 1)
    first, live = pos < first_len, pos < LEN_ALL
    parts = [msg_ref[j].astype(F32) for j in range(NHEAD)]
    sums = [p[64:65, :TOK] + p[65:66, :TOK] + p[66:67, :TOK] for p in parts]
    squares = [p[67:68, :TOK] + p[68:69, :TOK] + p[69:70, :TOK] for p in parts]
    mean, square = sums[0], squares[0]
    for j in range(1, NHEAD):
        mean, square = mean + sums[j], square + squares[j]
    mean, square = mean * (1.0 / D), square * (1.0 / D)
    var = square - mean * mean
    scaled, shifted = jnp.zeros((64, TOK), F32), jnp.zeros((64, 128), F32)
    for p, own in zip(parts, sums):
        scale_w = jnp.where(
            first,
            p[:64, TOK : TOK + 1] + p[:64, TOK + 4 : TOK + 5],
            p[:64, TOK + 1 : TOK + 2] + p[:64, TOK + 5 : TOK + 6],
        )
        scaled += p[:64, :TOK] + (own * (1.0 / 384) - mean) * scale_w
        shifted += p[:64]
    shift_w = jnp.where(
        first,
        shifted[:, TOK + 2 : TOK + 3] + shifted[:, TOK + 6 : TOK + 7],
        shifted[:, TOK + 3 : TOK + 4] + shifted[:, TOK + 7 : TOK + 8],
    )
    velocity = lax.rsqrt(var + EPSILON) * scaled + shift_w
    latent = lat_ref[...]

    def row_coef(i):
        return jnp.where(first, coef_ref[2 * i], coef_ref[2 * i + 1])

    root_a, root_1a, root_q, root_1q = (row_coef(i) for i in range(4))
    clean = root_a * latent - root_1a * velocity
    noise = root_1a * latent + root_a * velocity
    stepped = root_q * clean + root_1q * noise
    clean_ref[...] = jnp.where(live, clean, 0.0)
    prev_ref[...] = jnp.where(live, stepped, 0.0)


def alpha_table():
    betas = np.linspace(0.00085**0.5, 0.012**0.5, TRAIN_STEPS) ** 2
    return np.cumprod(1.0 - betas).astype(np.float32)


def request_of(position, first_len):
    return jnp.where(
        position < 0, -1, jnp.where(position < first_len, 0, jnp.where(position < LEN_ALL, 1, 2))
    )


def shards(
    lengths,
    step_index,
    query_act,
    key_act,
    value_act,
    hidden,
    attn_weight,
    gate_mod,
    shift_mod,
    scale_mod,
    proj_weight,
    latent,
):
    row, member = lax.axis_index("y"), lax.axis_index(("a", "c"))
    seq = row * (NA * NB) + member
    first_len = lengths[0]
    size = jnp.where(member < 12, 32, 48)
    part = jnp.where(member < 12, member % 3, member % 2)
    scal = jnp.stack([first_len, row, size, part * size, seq * TOK]).astype(jnp.int32)
    in_smem = pl.BlockSpec(memory_space=SMEM)
    big = pltpu.CompilerParams(vmem_limit_bytes=24 * 1024 * 1024)
    small = pltpu.CompilerParams(vmem_limit_bytes=8 * 1024 * 1024)

    any_vmem = pl.BlockSpec(memory_space=VMEM)

    packed = pl.pallas_call(
        pack_kernel, out_shape=jax.ShapeDtypeStruct((NG, TOK, 128), BF), name="pack"
    )(query_act, key_act, value_act)
    mine = lax.all_to_all(packed, ("a", "c"), 0, 0, tiled=True)
    keyvals = lax.all_gather(mine[:, HALF:].reshape(NG * HALF, 128), "y", axis=0, tiled=True)
    partial = pl.pallas_call(
        attend_kernel,
        out_shape=jax.ShapeDtypeStruct((NG, KEPT + 8, 128), BF),
        in_specs=[in_smem, any_vmem, any_vmem],
        out_specs=any_vmem,
        scratch_shapes=[
            VMEM((NY * KT, 256), BF),
            VMEM((NY, ROWS, KT), BF),
            VMEM((2, 256, QP), BF),
            VMEM((2, 8, QP), F32),
            VMEM((2, ROWS, QP), F32),
        ],
        compiler_params=big,
        name="attend",
    )(scal, mine, keyvals)
    parts = lax.all_to_all(partial, ("a", "c"), 0, 0, tiled=True)
    term = pl.pallas_call(
        merge_kernel,
        out_shape=jax.ShapeDtypeStruct((NHEAD, TOK, 384), BF),
        in_specs=[any_vmem, pl.BlockSpec(memory_space=pl.ANY)],
        out_specs=any_vmem,
        scratch_shapes=[VMEM((384, 128), F32), VMEM((384, D), BF), pltpu.SemaphoreType.DMA],
        compiler_params=big,
        name="merge",
    )(parts, attn_weight)
    terms = lax.all_to_all(term, ("x", "core"), 0, 0, tiled=True)
    hidden_out, message = pl.pallas_call(
        stream_kernel,
        out_shape=(
            jax.ShapeDtypeStruct((TOK, 384), BF),
            jax.ShapeDtypeStruct((NHEAD, 72, 128), BF),
        ),
        in_specs=[in_smem] + [any_vmem] * 6,
        compiler_params=small,
        name="stream",
    )(scal, terms, hidden, gate_mod, shift_mod, scale_mod, proj_weight.T)
    message = lax.all_to_all(message, ("x", "core"), 0, 0, tiled=True)
    table = jnp.asarray(alpha_table())
    alpha_now = table[step_index]
    alpha_prev = table[step_index - STEP_GAP]
    coef = jnp.concatenate(
        [
            jnp.sqrt(alpha_now),
            jnp.sqrt(1.0 - alpha_now),
            jnp.sqrt(alpha_prev),
            jnp.sqrt(1.0 - alpha_prev),
        ]
    )
    clean, stepped = pl.pallas_call(
        step_kernel,
        out_shape=(jax.ShapeDtypeStruct((64, TOK), F32),) * 2,
        in_specs=[in_smem, in_smem, any_vmem, any_vmem],
        compiler_params=small,
        name="ddim",
    )(scal, coef, message, latent.T)
    pairs = []
    for s in range(NY * NA * NB):
        for x in range(NX):
            up, down = (s * NX + x) * NC, (s * NX + x) * NC + 1
            if s + 1 < NY * NA * NB:
                pairs.append((up, up + NX * NC))
            if s > 0:
                pairs.append((down, down - NX * NC))
    got = lax.ppermute(stepped, ("y", "a", "c", "x", "core"), pairs)
    both = lax.all_gather(got, "core")
    offsets = jnp.arange(RIM, dtype=jnp.int32)
    start = seq * TOK
    lower_ok = request_of(start - RIM + offsets, first_len) == request_of(start, first_len)
    upper_ok = request_of(start + TOK + offsets, first_len) == request_of(
        start + TOK - 1, first_len
    )
    lower_ok &= start > 0
    upper_ok &= start + TOK < NY * NA * NB * TOK
    rims = jnp.concatenate(
        [
            jnp.where(lower_ok[None], both[0, :, TOK - RIM :], 0.0),
            jnp.where(upper_ok[None], both[1, :, :RIM], 0.0),
        ],
        axis=1,
    )
    return hidden_out, clean.T, stepped.T, rims.T


def solution(mesh):
    grid = Mesh(mesh.devices.reshape(NY, NA, NB, NX, NC), ("y", "a", "c", "x", "core"))
    seq, head = ("y", "a", "c"), ("x", "core")
    in_specs = (
        P(),
        P(),
        P(seq, head),
        P(seq, head),
        P(seq, head),
        P(seq, head),
        P(head, None),
        P(None, head),
        P(None, head),
        P(None, head),
        P(head, None),
        P(seq, None),
    )
    out_specs = (P(seq, head), P(seq, None), P(seq, None), P(seq, None))
    return jax.shard_map(shards, mesh=grid, in_specs=in_specs, out_specs=out_specs, check_vma=False)
```

```python
import jax
import jax.numpy as jnp
import numpy as np
from jax import lax
from jax.experimental import pallas as pl
from jax.experimental.pallas import tpu as pltpu
from jax.sharding import Mesh
from jax.sharding import PartitionSpec as P

D = 3072
HD = 64
RIM = 45
TOK = 96
HALF = 48
LEN_ALL = 5952
TRAIN_STEPS = 1000
STEP_GAP = 20
NY, NA, NB, NX, NC = 4, 4, 4, 4, 2
NG = NA * NB
NHEAD = 8
EPSILON = 1e-06
MASKED = -1e30
FLOOR = -0.5e30
HEAD_OF = (0, 0, 0, 1, 1, 1, 2, 2, 2, 3, 3, 3, 4, 4, 5, 5)
PART_OF = (0, 1, 2, 0, 1, 2, 0, 1, 2, 0, 1, 2, 0, 1, 0, 1)
SIZE_OF = (32,) * 12 + (48,) * 4
BF = jnp.bfloat16
F32 = jnp.float32
SMEM = pltpu.SMEM
VMEM = pltpu.VMEM


def low_lanes(rows):
    return lax.broadcasted_iota(jnp.int32, (rows, 128), 1) < HD


def swap(x):
    return pltpu.roll(x, HD, 1)


def pack_kernel(q_ref, k_ref, v_ref, out_ref):
    low_h, low_t = low_lanes(HALF), low_lanes(TOK)
    for pair in range(3):
        lanes = slice(128 * pair, 128 * pair + 128)
        q = q_ref[:, lanes].astype(F32) * 0.125
        k = k_ref[:, lanes].astype(F32)
        v = v_ref[:, lanes].astype(F32)
        top, bottom = q[:HALF], q[HALF:]
        queries = (jnp.where(low_h, top, swap(bottom)), jnp.where(low_h, swap(top), bottom))
        keyvals = (jnp.where(low_t, k, swap(v)), jnp.where(low_t, swap(k), v))
        for side in range(2):
            qh = queries[side].astype(BF)
            kvh = keyvals[side].astype(BF)
            for d in range(NG):
                if HEAD_OF[d] != 2 * pair + side:
                    continue
                size = SIZE_OF[d]
                start = PART_OF[d] * size
                out_ref[d, :HALF, :] = qh
                out_ref[d, HALF : HALF + size, :] = kvh[start : start + size]
                if size < HALF:
                    out_ref[d, HALF + size :, :] = jnp.zeros((HALF - size, 128), BF)


def pieces(x):
    hi = x.astype(BF).astype(F32)
    rest = x - hi
    mid = rest.astype(BF).astype(F32)
    return (hi, mid, rest - mid)


QT = NB * TOK
QP = 2 * QT
KT = NA * NB * HALF
KC = KT // 2
ROWS = 80
PART = KT // NA
KEPT = 48


def attend_kernel(scal_ref, q_ref, kv_ref, out_ref, key_ref, val_ref, query_ref, top_ref, acc_ref):
    first_len, size, offset = scal_ref[0], scal_ref[1], scal_ref[2]
    base, stride, by_row, by_part = scal_ref[4], scal_ref[5], scal_ref[6], scal_ref[7]
    row_tok = NA * NB * TOK
    lane3 = lax.broadcasted_iota(jnp.int32, (NA * NB, HALF, 128), 2)
    slot = lax.broadcasted_iota(jnp.int32, (NA * NB, HALF, 128), 1)
    block = lax.broadcasted_iota(jnp.int32, (NA * NB, HALF, 128), 0) * TOK + slot + offset
    block = jnp.where(slot < size, block, NY * row_tok)
    low = low_lanes(HALF)
    lane_q = lax.broadcasted_iota(jnp.int32, (16, QT), 1)
    row_q = lax.broadcasted_iota(jnp.int32, (16, QT), 0)
    ones = (lax.broadcasted_iota(jnp.int32, (ROWS - HD, KT), 0) == 0).astype(F32)
    for j in range(NY):
        own = jnp.where(block < first_len - j * row_tok, 0, jnp.where(block < LEN_ALL - j * row_tok, 1, 2))
        extra = jnp.where(lane3 == own, 1.0, 0.0)
        extra = extra.reshape(KT, 128).astype(BF)
        keyvals = jnp.concatenate(
            [
                kv_ref[pl.ds(pl.multiple_of((j * by_row + i * by_part) * PART, PART), PART), :]
                for i in range(NA)
            ],
            axis=0,
        )
        turned = keyvals.astype(F32).T
        key_ref[j * KT : (j + 1) * KT, :128] = keyvals
        key_ref[j * KT : (j + 1) * KT, 128:] = extra
        val_ref[j] = jnp.concatenate([turned[HD:], ones], axis=0).astype(BF)

        stack = []
        for c in range(NB):
            q = q_ref[j * NB + c, :HALF, :].astype(F32)
            stack += [jnp.where(low, q, 0.0), jnp.where(low, swap(q), 0.0)]
        pair, lanes = j // 2, slice(j % 2 * QT, j % 2 * QT + QT)
        query_ref[pair, :128, lanes] = jnp.concatenate(stack, axis=0).T.astype(BF)
        pos = lane_q + (base + j * stride)
        own = jnp.where(pos < first_len, 0, jnp.where(pos < LEN_ALL, 1, 2))
        query_ref[pair, 128:144, lanes] = jnp.where((row_q < 3) & ((row_q != own) | (own == 2)), MASKED, 0.0).astype(BF)
        query_ref[pair, 144:, lanes] = jnp.zeros((112, QT), BF)
    top_ref[...] = jnp.full_like(top_ref, FLOOR)
    acc_ref[...] = jnp.zeros_like(acc_ref)

    def holds(start, stop):
        stop = jnp.minimum(stop, LEN_ALL)
        return start < first_len, (stop > first_len) & (start < stop)

    def absorb(keys, values, t, lanes):
        scores = jnp.dot(keys, query_ref[t, :, lanes], preferred_element_type=F32)
        old = top_ref[t, :1, lanes]
        new = jnp.maximum(jnp.max(scores, axis=0, keepdims=True), old)
        weights = jnp.exp(scores - new).astype(BF)
        acc_ref[t, :, lanes] = acc_ref[t, :, lanes] * jnp.exp(old - new) + jnp.dot(
            values, weights, preferred_element_type=F32
        )
        top_ref[t, :, lanes] = jnp.broadcast_to(new, (8, new.shape[1]))

    def visit(number, carry):
        j, t = number // 2, number % 2

        def needed(half, side):
            start = base + (2 * t + side) * stride
            q_first, q_second = holds(start, start + QT)
            begin = j * row_tok + half * (row_tok // 2)
            k_first, k_second = holds(begin, begin + row_tok // 2)
            return (q_first & k_first) | (q_second & k_second)

        need = [[needed(half, side) for side in range(2)] for half in range(2)]
        every = need[0][0] & need[0][1] & need[1][0] & need[1][1]

        @pl.when(every)
        def _():
            rows = pl.ds(pl.multiple_of(j * KT, KT), KT)
            absorb(key_ref[rows, :], val_ref[j], t, slice(0, QP))

        @pl.when(jnp.logical_not(every))
        def _():
            for half in range(2):
                left, right = need[half]

                def take(lanes):
                    rows = pl.ds(pl.multiple_of(j * KT + half * KC, KC), KC)
                    values = val_ref[j, :, half * KC : (half + 1) * KC]
                    absorb(key_ref[rows, :], values, t, lanes)

                pl.when(left & right)(lambda: take(slice(0, QP)))
                pl.when(left & jnp.logical_not(right))(lambda: take(slice(0, QT)))
                pl.when(right & jnp.logical_not(left))(lambda: take(slice(QT, QP)))

        return carry

    lax.fori_loop(0, NY * 2, visit, 0)

    row8 = lax.broadcasted_iota(jnp.int32, (8, QT), 0)
    lane_m = lax.broadcasted_iota(jnp.int32, (KEPT, 128), 1)
    for t in range(NY):
        pair, lanes = t // 2, slice(t % 2 * QT, t % 2 * QT + QT)
        sums = acc_ref[pair, HD : HD + 1, lanes]
        stats = jnp.zeros((8, QT), F32)
        for number, piece in enumerate(pieces(top_ref[pair, :1, lanes]) + pieces(sums)):
            stats = jnp.where(row8 == number, piece, stats)
        whole = jnp.concatenate(
            [acc_ref[pair, :HD, lanes] * (1.0 / jnp.where(sums > 0.0, sums, 1.0)), stats], axis=0
        )
        for c in range(NB):
            moved = pltpu.roll(whole, QT - c * TOK, 1) if c else whole
            moved = moved[:, :128]
            rest = moved[KEPT:HD]
            thirds = [pltpu.roll(rest, (TOK - 32 * k) % 128, 1) for k in range(3)]
            kept = jnp.where(lane_m < TOK, moved[:KEPT], jnp.concatenate(thirds, axis=0))
            out_ref[t * NB + c] = jnp.concatenate([kept, moved[HD:]], axis=0).astype(BF)


def merge_kernel(part_ref, w_ref, out_ref, att_ref, copy_ref, sem):
    copy = pltpu.make_async_copy(w_ref, copy_ref, sem)
    copy.start()
    lane_r = lax.broadcasted_iota(jnp.int32, (HD - KEPT, 128), 1)
    stat = part_ref[:, KEPT:, :].astype(F32)
    tops = stat[:, 0] + stat[:, 1] + stat[:, 2]
    sums = stat[:, 3] + stat[:, 4] + stat[:, 5]
    for h in range(6):
        own = [d for d in range(NG) if HEAD_OF[d] == h]
        rows = slice(own[0], own[-1] + 1)
        top = jnp.max(tops[rows], axis=0, keepdims=True)
        scaled = jnp.exp(tops[rows] - top) * sums[rows]
        total = jnp.sum(scaled, axis=0, keepdims=True)
        shares = scaled / jnp.where(total > 0.0, total, 1.0)
        mixed = jnp.zeros((HD, 128), F32)
        for i, d in enumerate(own):
            part = part_ref[d, :KEPT, :].astype(F32)
            thirds = [
                pltpu.roll(part[16 * k : 16 * k + 16], (32 * k + 128 - TOK) % 128, 1)
                for k in range(3)
            ]
            rest = jnp.where(
                lane_r < 32, thirds[0], jnp.where(lane_r < 64, thirds[1], thirds[2])
            )
            mixed += shares[i : i + 1] * jnp.concatenate([part, rest], axis=0)
        att_ref[HD * h : HD * h + HD, :] = mixed
    attended = att_ref[...].T[:TOK].astype(BF)
    copy.wait()
    for j in range(NHEAD):
        out_ref[j] = jnp.dot(
            attended, copy_ref[:, 384 * j : 384 * j + 384], preferred_element_type=F32
        ).astype(BF)


def split2(x):
    hi = x.astype(BF)
    return hi, (x - hi.astype(F32)).astype(BF)


def stream_kernel(
    scal_ref, term_ref, hid_ref, gate_ref, shift_ref, scale_ref, w_ref, hid_out, msg_ref
):
    first_len, base = scal_ref[0], scal_ref[3]
    projected = term_ref[0].astype(F32)
    for j in range(1, NHEAD):
        projected += term_ref[j].astype(F32)
    pos = base + lax.broadcasted_iota(jnp.int32, (TOK, 384), 0)
    first, second = pos < first_len, pos < LEN_ALL

    def per_row(table):
        return jnp.where(first, table[0:1], jnp.where(second, table[1:2], 0.0))

    gate, shift = gate_ref[...].astype(F32), shift_ref[...].astype(F32)
    factor = 1.0 + scale_ref[...].astype(F32)
    x = (hid_ref[...].astype(F32) + per_row(gate) * projected).astype(BF)
    hid_out[...] = x
    xf = x.astype(F32)
    own_mean = jnp.sum(xf, axis=1, keepdims=True) * (1.0 / 384)
    scaled = jnp.concatenate(
        [(xf - own_mean) * per_row(factor), factor, shift, jnp.zeros((28, 384), F32)], axis=0
    )
    sq_hi, sq_lo = split2(xf * xf)
    ones = jnp.ones((8, 384), BF)

    def turn(left, right):
        return lax.dot_general(left, right, (((1,), (1,)), ((), ())), preferred_element_type=F32)

    high, rest = split2(scaled)
    w = w_ref[...]
    a = turn(w, high) + turn(w, rest)
    left = pltpu.roll(a - a.astype(BF).astype(F32), 4, 1)
    lane = lax.broadcasted_iota(jnp.int32, (64, 128), 1)
    a = jnp.where((lane >= TOK + 4) & (lane < TOK + 8), left, a).astype(BF)
    total = turn(ones, x)
    squares = turn(ones, sq_hi) + turn(ones, sq_lo)
    rows8 = lax.broadcasted_iota(jnp.int32, (8, TOK), 0)
    tail = jnp.zeros((8, TOK), F32)
    for number, piece in enumerate(pieces(total) + pieces(squares)):
        tail = jnp.where(rows8 == number, piece, tail)
    tail = jnp.concatenate([tail, jnp.zeros((8, 128 - TOK), F32)], axis=1)
    message = jnp.concatenate([a.astype(F32), tail], axis=0).astype(BF)
    for j in range(NHEAD):
        msg_ref[j] = message


def step_kernel(scal_ref, coef_ref, msg_ref, lat_ref, clean_ref, prev_ref):
    first_len, base = scal_ref[0], scal_ref[3]
    pos = base + lax.broadcasted_iota(jnp.int32, (64, TOK), 1)
    first, live = pos < first_len, pos < LEN_ALL
    parts = [msg_ref[j].astype(F32) for j in range(NHEAD)]
    sums = [p[64:65, :TOK] + p[65:66, :TOK] + p[66:67, :TOK] for p in parts]
    squares = [p[67:68, :TOK] + p[68:69, :TOK] + p[69:70, :TOK] for p in parts]
    mean, square = sums[0], squares[0]
    for j in range(1, NHEAD):
        mean, square = mean + sums[j], square + squares[j]
    mean, square = mean * (1.0 / D), square * (1.0 / D)
    var = square - mean * mean
    scaled, shifted = jnp.zeros((64, TOK), F32), jnp.zeros((64, 128), F32)
    for p, own in zip(parts, sums):
        scale_w = jnp.where(
            first,
            p[:64, TOK : TOK + 1] + p[:64, TOK + 4 : TOK + 5],
            p[:64, TOK + 1 : TOK + 2] + p[:64, TOK + 5 : TOK + 6],
        )
        scaled += p[:64, :TOK] + (own * (1.0 / 384) - mean) * scale_w
        shifted += p[:64]
    shift_w = jnp.where(
        first,
        shifted[:, TOK + 2 : TOK + 3] + shifted[:, TOK + 6 : TOK + 7],
        shifted[:, TOK + 3 : TOK + 4] + shifted[:, TOK + 7 : TOK + 8],
    )
    velocity = lax.rsqrt(var + EPSILON) * scaled + shift_w
    latent = lat_ref[...]

    def row_coef(i):
        return jnp.where(first, coef_ref[2 * i], coef_ref[2 * i + 1])

    root_a, root_1a, root_q, root_1q = (row_coef(i) for i in range(4))
    clean = root_a * latent - root_1a * velocity
    noise = root_1a * latent + root_a * velocity
    stepped = root_q * clean + root_1q * noise
    clean_ref[...] = jnp.where(live, clean, 0.0)
    prev_ref[...] = jnp.where(live, stepped, 0.0)


def alpha_table():
    betas = np.linspace(0.00085**0.5, 0.012**0.5, TRAIN_STEPS) ** 2
    return np.cumprod(1.0 - betas).astype(np.float32)


TOKEN_AXES = ("y", "a", "c", "core")
NEAR_Z = 1


def core_groups():
    def index(y, a, c, core):
        return ((y * NA + a) * NB + c) * NC + core

    near, far = [], []
    for core in range(NC):
        if core == NEAR_Z:
            near += [[index(y, a, c, core) for a in range(NA) for c in range(NB)] for y in range(NY)]
            far += [[index(y, a, c, core) for y in range(NY)] for a in range(NA) for c in range(NB)]
        else:
            near += [[index(y, a, c, core) for y in range(NY) for c in range(NB)] for a in range(NA)]
            far += [[index(y, a, c, core) for a in range(NA)] for y in range(NY) for c in range(NB)]
    return near, far


def request_of(position, first_len):
    return jnp.where(
        position < 0, -1, jnp.where(position < first_len, 0, jnp.where(position < LEN_ALL, 1, 2))
    )


def shards(
    lengths,
    step_index,
    query_act,
    key_act,
    value_act,
    hidden,
    attn_weight,
    gate_mod,
    shift_mod,
    scale_mod,
    proj_weight,
    latent,
):
    y, a, c = lax.axis_index("y"), lax.axis_index("a"), lax.axis_index("c")
    near_z = lax.axis_index("core") == NEAR_Z
    seq = (y * NA + a) * NB + c
    member = jnp.where(near_z, a, y) * NB + c
    first_len = lengths[0]
    size = jnp.where(member < 12, 32, 48)
    part = jnp.where(member < 12, member % 3, member % 2)
    row_tok, tile_tok = NA * NB * TOK, NB * TOK
    scal = jnp.stack(
        [
            first_len,
            size,
            part * size,
            seq * TOK,
            jnp.where(near_z, y * row_tok, a * tile_tok),
            jnp.where(near_z, tile_tok, row_tok),
            jnp.where(near_z, NA, 1),
            jnp.where(near_z, 1, NA),
        ]
    ).astype(jnp.int32)
    near, far = core_groups()
    in_smem = pl.BlockSpec(memory_space=SMEM)
    big = pltpu.CompilerParams(vmem_limit_bytes=24 * 1024 * 1024)
    small = pltpu.CompilerParams(vmem_limit_bytes=8 * 1024 * 1024)

    any_vmem = pl.BlockSpec(memory_space=VMEM)

    packed = pl.pallas_call(
        pack_kernel, out_shape=jax.ShapeDtypeStruct((NG, TOK, 128), BF), name="pack"
    )(query_act, key_act, value_act)
    mine = lax.all_to_all(packed, TOKEN_AXES, 0, 0, tiled=True, axis_index_groups=near)
    keyvals = lax.all_gather(
        mine[:, HALF:].reshape(NG * HALF, 128),
        TOKEN_AXES,
        axis=0,
        tiled=True,
        axis_index_groups=far,
    )
    partial = pl.pallas_call(
        attend_kernel,
        out_shape=jax.ShapeDtypeStruct((NG, KEPT + 8, 128), BF),
        in_specs=[in_smem, any_vmem, any_vmem],
        out_specs=any_vmem,
        scratch_shapes=[
            VMEM((NY * KT, 256), BF),
            VMEM((NY, ROWS, KT), BF),
            VMEM((2, 256, QP), BF),
            VMEM((2, 8, QP), F32),
            VMEM((2, ROWS, QP), F32),
        ],
        compiler_params=big,
        name="attend",
    )(scal, mine, keyvals)
    parts = lax.all_to_all(partial, TOKEN_AXES, 0, 0, tiled=True, axis_index_groups=near)
    term = pl.pallas_call(
        merge_kernel,
        out_shape=jax.ShapeDtypeStruct((NHEAD, TOK, 384), BF),
        in_specs=[any_vmem, pl.BlockSpec(memory_space=pl.ANY)],
        out_specs=any_vmem,
        scratch_shapes=[VMEM((384, 128), F32), VMEM((384, D), BF), pltpu.SemaphoreType.DMA],
        compiler_params=big,
        name="merge",
    )(parts, attn_weight)
    terms = lax.all_to_all(term, ("x", "core"), 0, 0, tiled=True)
    hidden_out, message = pl.pallas_call(
        stream_kernel,
        out_shape=(
            jax.ShapeDtypeStruct((TOK, 384), BF),
            jax.ShapeDtypeStruct((NHEAD, 72, 128), BF),
        ),
        in_specs=[in_smem] + [any_vmem] * 6,
        compiler_params=small,
        name="stream",
    )(scal, terms, hidden, gate_mod, shift_mod, scale_mod, proj_weight.T)
    message = lax.all_to_all(message, ("x", "core"), 0, 0, tiled=True)
    table = jnp.asarray(alpha_table())
    alpha_now = table[step_index]
    alpha_prev = table[step_index - STEP_GAP]
    coef = jnp.concatenate(
        [
            jnp.sqrt(alpha_now),
            jnp.sqrt(1.0 - alpha_now),
            jnp.sqrt(alpha_prev),
            jnp.sqrt(1.0 - alpha_prev),
        ]
    )
    clean, stepped = pl.pallas_call(
        step_kernel,
        out_shape=(jax.ShapeDtypeStruct((64, TOK), F32),) * 2,
        in_specs=[in_smem, in_smem, any_vmem, any_vmem],
        compiler_params=small,
        name="ddim",
    )(scal, coef, message, latent.T)
    pairs = []
    for s in range(NY * NA * NB):
        for x in range(NX):
            up, down = (s * NX + x) * NC, (s * NX + x) * NC + 1
            if s + 1 < NY * NA * NB:
                pairs.append((up, up + NX * NC))
            if s > 0:
                pairs.append((down, down - NX * NC))
    got = lax.ppermute(stepped, ("y", "a", "c", "x", "core"), pairs)
    both = lax.all_gather(got, "core")
    offsets = jnp.arange(RIM, dtype=jnp.int32)
    start = seq * TOK
    lower_ok = request_of(start - RIM + offsets, first_len) == request_of(start, first_len)
    upper_ok = request_of(start + TOK + offsets, first_len) == request_of(
        start + TOK - 1, first_len
    )
    lower_ok &= start > 0
    upper_ok &= start + TOK < NY * NA * NB * TOK
    rims = jnp.concatenate(
        [
            jnp.where(lower_ok[None], both[0, :, TOK - RIM :], 0.0),
            jnp.where(upper_ok[None], both[1, :, :RIM], 0.0),
        ],
        axis=1,
    )
    return hidden_out, clean.T, stepped.T, rims.T


def solution(mesh):
    grid = Mesh(mesh.devices.reshape(NY, NA, NB, NX, NC), ("y", "a", "c", "x", "core"))
    seq, head = ("y", "a", "c"), ("x", "core")
    in_specs = (
        P(),
        P(),
        P(seq, head),
        P(seq, head),
        P(seq, head),
        P(seq, head),
        P(head, None),
        P(None, head),
        P(None, head),
        P(None, head),
        P(head, None),
        P(seq, None),
    )
    out_specs = (P(seq, head), P(seq, None), P(seq, None), P(seq, None))
    return jax.shard_map(shards, mesh=grid, in_specs=in_specs, out_specs=out_specs, check_vma=False)
```

```python
import jax
import jax.numpy as jnp
import numpy as np
from jax import lax
from jax.experimental import pallas as pl
from jax.experimental.pallas import tpu as pltpu
from jax.sharding import Mesh
from jax.sharding import PartitionSpec as P

D = 3072
HD = 64
RIM = 45
TOK = 96
HALF = 48
LEN_ALL = 5952
TRAIN_STEPS = 1000
STEP_GAP = 20
NY, NA, NB, NX, NC = 4, 4, 4, 4, 2
NG = NA * NB
NHEAD = 8
EPSILON = 1e-06
MASKED = -1e30
FLOOR = -0.5e30
HEAD_OF = (0, 0, 0, 1, 1, 1, 2, 2, 2, 3, 3, 3, 4, 4, 5, 5)
PART_OF = (0, 1, 2, 0, 1, 2, 0, 1, 2, 0, 1, 2, 0, 1, 0, 1)
SIZE_OF = (32,) * 12 + (48,) * 4
BF = jnp.bfloat16
F32 = jnp.float32
SMEM = pltpu.SMEM
VMEM = pltpu.VMEM


def low_lanes(rows):
    return lax.broadcasted_iota(jnp.int32, (rows, 128), 1) < HD


def swap(x):
    return pltpu.roll(x, HD, 1)


def pack_kernel(q_ref, k_ref, v_ref, out_ref):
    low_h, low_t = low_lanes(HALF), low_lanes(TOK)
    for pair in range(3):
        lanes = slice(128 * pair, 128 * pair + 128)
        q = q_ref[:, lanes].astype(F32) * 0.125
        k = k_ref[:, lanes].astype(F32)
        v = v_ref[:, lanes].astype(F32)
        top, bottom = q[:HALF], q[HALF:]
        queries = (jnp.where(low_h, top, swap(bottom)), jnp.where(low_h, swap(top), bottom))
        keyvals = (jnp.where(low_t, k, swap(v)), jnp.where(low_t, swap(k), v))
        for side in range(2):
            qh = queries[side].astype(BF)
            kvh = keyvals[side].astype(BF)
            for d in range(NG):
                if HEAD_OF[d] != 2 * pair + side:
                    continue
                size = SIZE_OF[d]
                start = PART_OF[d] * size
                out_ref[d, :HALF, :] = qh
                out_ref[d, HALF : HALF + size, :] = kvh[start : start + size]
                if size < HALF:
                    out_ref[d, HALF + size :, :] = jnp.zeros((HALF - size, 128), BF)


def pieces(x):
    hi = x.astype(BF).astype(F32)
    rest = x - hi
    mid = rest.astype(BF).astype(F32)
    return (hi, mid, rest - mid)


QT = NB * TOK
QP = 2 * QT
KT = NA * NB * HALF
KC = KT // 2
ROWS = 80
PART = KT // NA
KEPT = 48


def attend_kernel(scal_ref, q_ref, kv_ref, out_ref, key_ref, val_ref, query_ref, top_ref, acc_ref):
    first_len, size, offset = scal_ref[0], scal_ref[1], scal_ref[2]
    base, stride, by_row, by_part = scal_ref[4], scal_ref[5], scal_ref[6], scal_ref[7]
    row_tok = NA * NB * TOK
    lane3 = lax.broadcasted_iota(jnp.int32, (NA * NB, HALF, 128), 2)
    slot = lax.broadcasted_iota(jnp.int32, (NA * NB, HALF, 128), 1)
    block = lax.broadcasted_iota(jnp.int32, (NA * NB, HALF, 128), 0) * TOK + slot + offset
    block = jnp.where(slot < size, block, NY * row_tok)
    low = low_lanes(HALF)
    lane_q = lax.broadcasted_iota(jnp.int32, (16, QT), 1)
    row_q = lax.broadcasted_iota(jnp.int32, (16, QT), 0)
    ones = (lax.broadcasted_iota(jnp.int32, (ROWS - HD, KT), 0) == 0).astype(F32)
    for j in range(NY):
        own = jnp.where(block < first_len - j * row_tok, 0, jnp.where(block < LEN_ALL - j * row_tok, 1, 2))
        extra = jnp.where(lane3 == own, 1.0, 0.0)
        extra = extra.reshape(KT, 128).astype(BF)
        keyvals = jnp.concatenate(
            [
                kv_ref[pl.ds(pl.multiple_of((j * by_row + i * by_part) * PART, PART), PART), :]
                for i in range(NA)
            ],
            axis=0,
        )
        turned = keyvals.astype(F32).T
        key_ref[j * KT : (j + 1) * KT, :128] = keyvals
        key_ref[j * KT : (j + 1) * KT, 128:] = extra
        val_ref[j] = jnp.concatenate([turned[HD:], ones], axis=0).astype(BF)

        stack = []
        for c in range(NB):
            q = q_ref[j * NB + c, :HALF, :].astype(F32)
            stack += [jnp.where(low, q, 0.0), jnp.where(low, swap(q), 0.0)]
        pair, lanes = j // 2, slice(j % 2 * QT, j % 2 * QT + QT)
        query_ref[pair, :128, lanes] = jnp.concatenate(stack, axis=0).T.astype(BF)
        pos = lane_q + (base + j * stride)
        own = jnp.where(pos < first_len, 0, jnp.where(pos < LEN_ALL, 1, 2))
        query_ref[pair, 128:144, lanes] = jnp.where((row_q < 3) & ((row_q != own) | (own == 2)), MASKED, 0.0).astype(BF)
        query_ref[pair, 144:, lanes] = jnp.zeros((112, QT), BF)
    top_ref[...] = jnp.full_like(top_ref, FLOOR)
    acc_ref[...] = jnp.zeros_like(acc_ref)

    def holds(start, stop):
        stop = jnp.minimum(stop, LEN_ALL)
        return start < first_len, (stop > first_len) & (start < stop)

    def absorb(keys, values, t, lanes):
        scores = jnp.dot(keys, query_ref[t, :, lanes], preferred_element_type=F32)
        old = top_ref[t, :1, lanes]
        new = jnp.maximum(jnp.max(scores, axis=0, keepdims=True), old)
        weights = jnp.exp(scores - new).astype(BF)
        acc_ref[t, :, lanes] = acc_ref[t, :, lanes] * jnp.exp(old - new) + jnp.dot(
            values, weights, preferred_element_type=F32
        )
        top_ref[t, :, lanes] = jnp.broadcast_to(new, (8, new.shape[1]))

    def visit(number, carry):
        j, t = number // 2, number % 2

        def needed(half, side):
            start = base + (2 * t + side) * stride
            q_first, q_second = holds(start, start + QT)
            begin = j * row_tok + half * (row_tok // 2)
            k_first, k_second = holds(begin, begin + row_tok // 2)
            return (q_first & k_first) | (q_second & k_second)

        need = [[needed(half, side) for side in range(2)] for half in range(2)]
        lefts, rights = need[0][0] & need[1][0], need[0][1] & need[1][1]
        no_left = jnp.logical_not(need[0][0] | need[1][0])
        no_right = jnp.logical_not(need[0][1] | need[1][1])
        rows = pl.ds(pl.multiple_of(j * KT, KT), KT)

        def whole_chunk(lanes):
            absorb(key_ref[rows, :], val_ref[j], t, lanes)

        pl.when(lefts & rights)(lambda: whole_chunk(slice(0, QP)))
        pl.when(lefts & no_right)(lambda: whole_chunk(slice(0, QT)))
        pl.when(rights & no_left)(lambda: whole_chunk(slice(QT, QP)))
        done = (lefts & rights) | (lefts & no_right) | (rights & no_left)

        @pl.when(jnp.logical_not(done))
        def _():
            for half in range(2):
                left, right = need[half]

                def take(lanes):
                    rows = pl.ds(pl.multiple_of(j * KT + half * KC, KC), KC)
                    values = val_ref[j, :, half * KC : (half + 1) * KC]
                    absorb(key_ref[rows, :], values, t, lanes)

                pl.when(left & right)(lambda: take(slice(0, QP)))
                pl.when(left & jnp.logical_not(right))(lambda: take(slice(0, QT)))
                pl.when(right & jnp.logical_not(left))(lambda: take(slice(QT, QP)))

        return carry

    lax.fori_loop(0, NY * 2, visit, 0)

    row8 = lax.broadcasted_iota(jnp.int32, (8, QT), 0)
    lane_m = lax.broadcasted_iota(jnp.int32, (KEPT, 128), 1)
    for t in range(NY):
        pair, lanes = t // 2, slice(t % 2 * QT, t % 2 * QT + QT)
        sums = acc_ref[pair, HD : HD + 1, lanes]
        stats = jnp.zeros((8, QT), F32)
        for number, piece in enumerate(pieces(top_ref[pair, :1, lanes]) + pieces(sums)):
            stats = jnp.where(row8 == number, piece, stats)
        whole = jnp.concatenate(
            [acc_ref[pair, :HD, lanes] * (1.0 / jnp.where(sums > 0.0, sums, 1.0)), stats], axis=0
        )
        for c in range(NB):
            skip = c * TOK // 128 * 128
            moved = whole[:, skip : min(skip + 256, QT)]
            if c:
                moved = pltpu.roll(moved, moved.shape[1] - (c * TOK - skip), 1)
            moved = moved[:, :128]
            rest = moved[KEPT:HD]
            thirds = [pltpu.roll(rest, (TOK - 32 * k) % 128, 1) for k in range(3)]
            kept = jnp.where(lane_m < TOK, moved[:KEPT], jnp.concatenate(thirds, axis=0))
            out_ref[t * NB + c] = jnp.concatenate([kept, moved[HD:]], axis=0).astype(BF)


def merge_kernel(part_ref, w_ref, out_ref, att_ref):
    lane_r = lax.broadcasted_iota(jnp.int32, (HD - KEPT, 128), 1)
    stat = part_ref[:, KEPT:, :].astype(F32)
    tops = stat[:, 0] + stat[:, 1] + stat[:, 2]
    sums = stat[:, 3] + stat[:, 4] + stat[:, 5]
    for h in range(6):
        own = [d for d in range(NG) if HEAD_OF[d] == h]
        rows = slice(own[0], own[-1] + 1)
        top = jnp.max(tops[rows], axis=0, keepdims=True)
        scaled = jnp.exp(tops[rows] - top) * sums[rows]
        total = jnp.sum(scaled, axis=0, keepdims=True)
        shares = scaled / jnp.where(total > 0.0, total, 1.0)
        mixed = jnp.zeros((HD, 128), F32)
        for i, d in enumerate(own):
            part = part_ref[d, :KEPT, :].astype(F32)
            thirds = [
                pltpu.roll(part[16 * k : 16 * k + 16], (32 * k + 128 - TOK) % 128, 1)
                for k in range(3)
            ]
            rest = jnp.where(
                lane_r < 32, thirds[0], jnp.where(lane_r < 64, thirds[1], thirds[2])
            )
            mixed += shares[i : i + 1] * jnp.concatenate([part, rest], axis=0)
        att_ref[HD * h : HD * h + HD, :] = mixed
    attended = att_ref[...].T[:TOK].astype(BF)
    for j in range(NHEAD):
        out_ref[j] = jnp.dot(
            attended, w_ref[:, 384 * j : 384 * j + 384], preferred_element_type=F32
        ).astype(BF)


def split2(x):
    hi = x.astype(BF)
    return hi, (x - hi.astype(F32)).astype(BF)


def stream_kernel(
    scal_ref, term_ref, hid_ref, gate_ref, shift_ref, scale_ref, w_ref, hid_out, msg_ref
):
    first_len, base = scal_ref[0], scal_ref[3]
    projected = term_ref[0].astype(F32)
    for j in range(1, NHEAD):
        projected += term_ref[j].astype(F32)
    pos = base + lax.broadcasted_iota(jnp.int32, (TOK, 384), 0)
    first, second = pos < first_len, pos < LEN_ALL

    def per_row(table):
        return jnp.where(first, table[0:1], jnp.where(second, table[1:2], 0.0))

    gate, shift = gate_ref[...].astype(F32), shift_ref[...].astype(F32)
    factor = 1.0 + scale_ref[...].astype(F32)
    x = (hid_ref[...].astype(F32) + per_row(gate) * projected).astype(BF)
    hid_out[...] = x
    xf = x.astype(F32)
    own_mean = jnp.sum(xf, axis=1, keepdims=True) * (1.0 / 384)
    scaled = jnp.concatenate(
        [(xf - own_mean) * per_row(factor), factor, shift, jnp.zeros((28, 384), F32)], axis=0
    )
    sq_hi, sq_lo = split2(xf * xf)
    ones = jnp.ones((8, 384), BF)

    def turn(left, right):
        return lax.dot_general(left, right, (((1,), (1,)), ((), ())), preferred_element_type=F32)

    high, rest = split2(scaled)
    w = w_ref[...]
    a = turn(w, high) + turn(w, rest)
    left = pltpu.roll(a - a.astype(BF).astype(F32), 4, 1)
    lane = lax.broadcasted_iota(jnp.int32, (64, 128), 1)
    a = jnp.where((lane >= TOK + 4) & (lane < TOK + 8), left, a).astype(BF)
    total = turn(ones, x)
    squares = turn(ones, sq_hi) + turn(ones, sq_lo)
    rows8 = lax.broadcasted_iota(jnp.int32, (8, TOK), 0)
    tail = jnp.zeros((8, TOK), F32)
    for number, piece in enumerate(pieces(total) + pieces(squares)):
        tail = jnp.where(rows8 == number, piece, tail)
    tail = jnp.concatenate([tail, jnp.zeros((8, 128 - TOK), F32)], axis=1)
    message = jnp.concatenate([a.astype(F32), tail], axis=0).astype(BF)
    for j in range(NHEAD):
        msg_ref[j] = message


def step_kernel(scal_ref, coef_ref, msg_ref, lat_ref, clean_ref, prev_ref):
    first_len, base = scal_ref[0], scal_ref[3]
    pos = base + lax.broadcasted_iota(jnp.int32, (64, TOK), 1)
    first, live = pos < first_len, pos < LEN_ALL
    parts = [msg_ref[j].astype(F32) for j in range(NHEAD)]
    sums = [p[64:65, :TOK] + p[65:66, :TOK] + p[66:67, :TOK] for p in parts]
    squares = [p[67:68, :TOK] + p[68:69, :TOK] + p[69:70, :TOK] for p in parts]
    mean, square = sums[0], squares[0]
    for j in range(1, NHEAD):
        mean, square = mean + sums[j], square + squares[j]
    mean, square = mean * (1.0 / D), square * (1.0 / D)
    var = square - mean * mean
    scaled, shifted = jnp.zeros((64, TOK), F32), jnp.zeros((64, 128), F32)
    for p, own in zip(parts, sums):
        scale_w = jnp.where(
            first,
            p[:64, TOK : TOK + 1] + p[:64, TOK + 4 : TOK + 5],
            p[:64, TOK + 1 : TOK + 2] + p[:64, TOK + 5 : TOK + 6],
        )
        scaled += p[:64, :TOK] + (own * (1.0 / 384) - mean) * scale_w
        shifted += p[:64]
    shift_w = jnp.where(
        first,
        shifted[:, TOK + 2 : TOK + 3] + shifted[:, TOK + 6 : TOK + 7],
        shifted[:, TOK + 3 : TOK + 4] + shifted[:, TOK + 7 : TOK + 8],
    )
    velocity = lax.rsqrt(var + EPSILON) * scaled + shift_w
    latent = lat_ref[...]

    def row_coef(i):
        return jnp.where(first, coef_ref[2 * i], coef_ref[2 * i + 1])

    root_a, root_1a, root_q, root_1q = (row_coef(i) for i in range(4))
    clean = root_a * latent - root_1a * velocity
    noise = root_1a * latent + root_a * velocity
    stepped = root_q * clean + root_1q * noise
    clean_ref[...] = jnp.where(live, clean, 0.0)
    prev_ref[...] = jnp.where(live, stepped, 0.0)


def alpha_table():
    betas = np.linspace(0.00085**0.5, 0.012**0.5, TRAIN_STEPS) ** 2
    return np.cumprod(1.0 - betas).astype(np.float32)


TOKEN_AXES = ("y", "a", "c", "core")
NEAR_Z = 1


def core_groups():
    def index(y, a, c, core):
        return ((y * NA + a) * NB + c) * NC + core

    near, far = [], []
    for core in range(NC):
        if core == NEAR_Z:
            near += [[index(y, a, c, core) for a in range(NA) for c in range(NB)] for y in range(NY)]
            far += [[index(y, a, c, core) for y in range(NY)] for a in range(NA) for c in range(NB)]
        else:
            near += [[index(y, a, c, core) for y in range(NY) for c in range(NB)] for a in range(NA)]
            far += [[index(y, a, c, core) for a in range(NA)] for y in range(NY) for c in range(NB)]
    return near, far


def request_of(position, first_len):
    return jnp.where(
        position < 0, -1, jnp.where(position < first_len, 0, jnp.where(position < LEN_ALL, 1, 2))
    )


def shards(
    lengths,
    step_index,
    query_act,
    key_act,
    value_act,
    hidden,
    attn_weight,
    gate_mod,
    shift_mod,
    scale_mod,
    proj_weight,
    latent,
):
    y, a, c = lax.axis_index("y"), lax.axis_index("a"), lax.axis_index("c")
    near_z = lax.axis_index("core") == NEAR_Z
    seq = (y * NA + a) * NB + c
    member = jnp.where(near_z, a, y) * NB + c
    first_len = lengths[0]
    size = jnp.where(member < 12, 32, 48)
    part = jnp.where(member < 12, member % 3, member % 2)
    row_tok, tile_tok = NA * NB * TOK, NB * TOK
    scal = jnp.stack(
        [
            first_len,
            size,
            part * size,
            seq * TOK,
            jnp.where(near_z, y * row_tok, a * tile_tok),
            jnp.where(near_z, tile_tok, row_tok),
            jnp.where(near_z, NA, 1),
            jnp.where(near_z, 1, NA),
        ]
    ).astype(jnp.int32)
    near, far = core_groups()
    in_smem = pl.BlockSpec(memory_space=SMEM)
    big = pltpu.CompilerParams(vmem_limit_bytes=24 * 1024 * 1024)
    small = pltpu.CompilerParams(vmem_limit_bytes=8 * 1024 * 1024)

    any_vmem = pl.BlockSpec(memory_space=VMEM)

    packed = pl.pallas_call(
        pack_kernel, out_shape=jax.ShapeDtypeStruct((NG, TOK, 128), BF), name="pack"
    )(query_act, key_act, value_act)
    mine = lax.all_to_all(packed, TOKEN_AXES, 0, 0, tiled=True, axis_index_groups=near)
    keyvals = lax.all_gather(
        mine[:, HALF:].reshape(NG * HALF, 128),
        TOKEN_AXES,
        axis=0,
        tiled=True,
        axis_index_groups=far,
    )
    partial = pl.pallas_call(
        attend_kernel,
        out_shape=jax.ShapeDtypeStruct((NG, KEPT + 8, 128), BF),
        in_specs=[in_smem, any_vmem, any_vmem],
        out_specs=any_vmem,
        scratch_shapes=[
            VMEM((NY * KT, 256), BF),
            VMEM((NY, ROWS, KT), BF),
            VMEM((2, 256, QP), BF),
            VMEM((2, 8, QP), F32),
            VMEM((2, ROWS, QP), F32),
        ],
        compiler_params=big,
        name="attend",
    )(scal, mine, keyvals)
    parts = lax.all_to_all(partial, TOKEN_AXES, 0, 0, tiled=True, axis_index_groups=near)
    term = pl.pallas_call(
        merge_kernel,
        out_shape=jax.ShapeDtypeStruct((NHEAD, TOK, 384), BF),
        in_specs=[any_vmem, any_vmem],
        out_specs=any_vmem,
        scratch_shapes=[VMEM((384, 128), F32)],
        compiler_params=big,
        name="merge",
    )(parts, attn_weight)
    terms = lax.all_to_all(term, ("x", "core"), 0, 0, tiled=True)
    hidden_out, message = pl.pallas_call(
        stream_kernel,
        out_shape=(
            jax.ShapeDtypeStruct((TOK, 384), BF),
            jax.ShapeDtypeStruct((NHEAD, 72, 128), BF),
        ),
        in_specs=[in_smem] + [any_vmem] * 6,
        compiler_params=small,
        name="stream",
    )(scal, terms, hidden, gate_mod, shift_mod, scale_mod, proj_weight.T)
    message = lax.all_to_all(message, ("x", "core"), 0, 0, tiled=True)
    table = jnp.asarray(alpha_table())
    alpha_now = table[step_index]
    alpha_prev = table[step_index - STEP_GAP]
    coef = jnp.concatenate(
        [
            jnp.sqrt(alpha_now),
            jnp.sqrt(1.0 - alpha_now),
            jnp.sqrt(alpha_prev),
            jnp.sqrt(1.0 - alpha_prev),
        ]
    )
    clean, stepped = pl.pallas_call(
        step_kernel,
        out_shape=(jax.ShapeDtypeStruct((64, TOK), F32),) * 2,
        in_specs=[in_smem, in_smem, any_vmem, any_vmem],
        compiler_params=small,
        name="ddim",
    )(scal, coef, message, latent.T)
    pairs = []
    for s in range(NY * NA * NB):
        for x in range(NX):
            up, down = (s * NX + x) * NC, (s * NX + x) * NC + 1
            if s + 1 < NY * NA * NB:
                pairs.append((up, up + NX * NC))
            if s > 0:
                pairs.append((down, down - NX * NC))
    got = lax.ppermute(stepped, ("y", "a", "c", "x", "core"), pairs)
    both = lax.all_gather(got, "core")
    offsets = jnp.arange(RIM, dtype=jnp.int32)
    start = seq * TOK
    lower_ok = request_of(start - RIM + offsets, first_len) == request_of(start, first_len)
    upper_ok = request_of(start + TOK + offsets, first_len) == request_of(
        start + TOK - 1, first_len
    )
    lower_ok &= start > 0
    upper_ok &= start + TOK < NY * NA * NB * TOK
    rims = jnp.concatenate(
        [
            jnp.where(lower_ok[None], both[0, :, TOK - RIM :], 0.0),
            jnp.where(upper_ok[None], both[1, :, :RIM], 0.0),
        ],
        axis=1,
    )
    return hidden_out, clean.T, stepped.T, rims.T


def solution(mesh):
    grid = Mesh(mesh.devices.reshape(NY, NA, NB, NX, NC), ("y", "a", "c", "x", "core"))
    seq, head = ("y", "a", "c"), ("x", "core")
    in_specs = (
        P(),
        P(),
        P(seq, head),
        P(seq, head),
        P(seq, head),
        P(seq, head),
        P(head, None),
        P(None, head),
        P(None, head),
        P(None, head),
        P(head, None),
        P(seq, None),
    )
    out_specs = (P(seq, head), P(seq, None), P(seq, None), P(seq, None))
    return jax.shard_map(shards, mesh=grid, in_specs=in_specs, out_specs=out_specs, check_vma=False)
```

```python
import jax
import jax.numpy as jnp
import numpy as np
from jax import lax
from jax.experimental import pallas as pl
from jax.experimental.pallas import tpu as pltpu
from jax.sharding import Mesh
from jax.sharding import PartitionSpec as P

D = 3072
HD = 64
RIM = 45
TOK = 96
HALF = 48
LEN_ALL = 5952
TRAIN_STEPS = 1000
STEP_GAP = 20
NY, NA, NB, NX, NC = 4, 4, 4, 4, 2
NG = NA * NB
NHEAD = 8
EPSILON = 1e-06
MASKED = -1e30
FLOOR = -0.5e30
HEAD_OF = (0, 0, 0, 1, 1, 1, 2, 2, 2, 3, 3, 3, 4, 4, 5, 5)
PART_OF = (0, 1, 2, 0, 1, 2, 0, 1, 2, 0, 1, 2, 0, 1, 0, 1)
SIZE_OF = (32,) * 12 + (48,) * 4
BF = jnp.bfloat16
F32 = jnp.float32
SMEM = pltpu.SMEM
VMEM = pltpu.VMEM


def low_lanes(rows):
    return lax.broadcasted_iota(jnp.int32, (rows, 128), 1) < HD


def swap(x):
    return pltpu.roll(x, HD, 1)


def pack_kernel(q_ref, k_ref, v_ref, out_ref):
    low_h, low_t = low_lanes(HALF), low_lanes(TOK)
    for pair in range(3):
        lanes = slice(128 * pair, 128 * pair + 128)
        q = q_ref[:, lanes].astype(F32) * 0.125
        k = k_ref[:, lanes].astype(F32)
        v = v_ref[:, lanes].astype(F32)
        top, bottom = q[:HALF], q[HALF:]
        queries = (jnp.where(low_h, top, swap(bottom)), jnp.where(low_h, swap(top), bottom))
        keyvals = (jnp.where(low_t, k, swap(v)), jnp.where(low_t, swap(k), v))
        for side in range(2):
            qh = queries[side].astype(BF)
            kvh = keyvals[side].astype(BF)
            for d in range(NG):
                if HEAD_OF[d] != 2 * pair + side:
                    continue
                size = SIZE_OF[d]
                start = PART_OF[d] * size
                out_ref[d, :HALF, :] = qh
                out_ref[d, HALF : HALF + size, :] = kvh[start : start + size]
                if size < HALF:
                    out_ref[d, HALF + size :, :] = jnp.zeros((HALF - size, 128), BF)


def pieces(x):
    hi = x.astype(BF).astype(F32)
    rest = x - hi
    mid = rest.astype(BF).astype(F32)
    return (hi, mid, rest - mid)


QT = NB * TOK
QP = 2 * QT
KT = NA * NB * HALF
KC = KT // 2
ROWS = 80
PART = KT // NA
KEPT = 48


def attend_kernel(scal_ref, q_ref, kv_ref, out_ref, key_ref, val_ref, query_ref, top_ref, acc_ref):
    first_len, size, offset = scal_ref[0], scal_ref[1], scal_ref[2]
    base, stride, by_row, by_part = scal_ref[4], scal_ref[5], scal_ref[6], scal_ref[7]
    row_tok = NA * NB * TOK
    lane3 = lax.broadcasted_iota(jnp.int32, (NA * NB, HALF, 128), 2)
    slot = lax.broadcasted_iota(jnp.int32, (NA * NB, HALF, 128), 1)
    block = lax.broadcasted_iota(jnp.int32, (NA * NB, HALF, 128), 0) * TOK + slot + offset
    block = jnp.where(slot < size, block, NY * row_tok)
    low = low_lanes(HALF)
    lane_q = lax.broadcasted_iota(jnp.int32, (16, QT), 1)
    row_q = lax.broadcasted_iota(jnp.int32, (16, QT), 0)
    ones = (lax.broadcasted_iota(jnp.int32, (ROWS - HD, KT), 0) == 0).astype(F32)
    for j in range(NY):
        own = jnp.where(block < first_len - j * row_tok, 0, jnp.where(block < LEN_ALL - j * row_tok, 1, 2))
        extra = jnp.where(lane3 == own, 1.0, 0.0)
        extra = extra.reshape(KT, 128).astype(BF)
        keyvals = jnp.concatenate(
            [
                kv_ref[pl.ds(pl.multiple_of((j * by_row + i * by_part) * PART, PART), PART), :]
                for i in range(NA)
            ],
            axis=0,
        )
        turned = keyvals.astype(F32).T
        key_ref[j * KT : (j + 1) * KT, :128] = keyvals
        key_ref[j * KT : (j + 1) * KT, 128:] = extra
        val_ref[j] = jnp.concatenate([turned[HD:], ones], axis=0).astype(BF)

        stack = []
        for c in range(NB):
            q = q_ref[j * NB + c, :HALF, :].astype(F32)
            stack += [jnp.where(low, q, 0.0), jnp.where(low, swap(q), 0.0)]
        pair, lanes = j // 2, slice(j % 2 * QT, j % 2 * QT + QT)
        query_ref[pair, :128, lanes] = jnp.concatenate(stack, axis=0).T.astype(BF)
        pos = lane_q + (base + j * stride)
        own = jnp.where(pos < first_len, 0, jnp.where(pos < LEN_ALL, 1, 2))
        query_ref[pair, 128:144, lanes] = jnp.where((row_q < 3) & ((row_q != own) | (own == 2)), MASKED, 0.0).astype(BF)
        query_ref[pair, 144:, lanes] = jnp.zeros((112, QT), BF)
    top_ref[...] = jnp.full_like(top_ref, FLOOR)
    acc_ref[...] = jnp.zeros_like(acc_ref)

    def holds(start, stop):
        stop = jnp.minimum(stop, LEN_ALL)
        return start < first_len, (stop > first_len) & (start < stop)

    def absorb(keys, values, t, lanes):
        scores = jnp.dot(keys, query_ref[t, :, lanes], preferred_element_type=F32)
        old = top_ref[t, :1, lanes]
        new = jnp.maximum(jnp.max(scores, axis=0, keepdims=True), old)
        weights = jnp.exp(scores - new).astype(BF)
        acc_ref[t, :, lanes] = acc_ref[t, :, lanes] * jnp.exp(old - new) + jnp.dot(
            values, weights, preferred_element_type=F32
        )
        top_ref[t, :, lanes] = jnp.broadcast_to(new, (8, new.shape[1]))

    def visit(number, carry):
        j, t = number // 2, number % 2

        def needed(half, side):
            start = base + (2 * t + side) * stride
            q_first, q_second = holds(start, start + QT)
            begin = j * row_tok + half * (row_tok // 2)
            k_first, k_second = holds(begin, begin + row_tok // 2)
            return (q_first & k_first) | (q_second & k_second)

        need = [[needed(half, side) for side in range(2)] for half in range(2)]
        lefts, rights = need[0][0] & need[1][0], need[0][1] & need[1][1]
        no_left = jnp.logical_not(need[0][0] | need[1][0])
        no_right = jnp.logical_not(need[0][1] | need[1][1])
        rows = pl.ds(pl.multiple_of(j * KT, KT), KT)

        def whole_chunk(lanes):
            absorb(key_ref[rows, :], val_ref[j], t, lanes)

        pl.when(lefts & rights)(lambda: whole_chunk(slice(0, QP)))
        pl.when(lefts & no_right)(lambda: whole_chunk(slice(0, QT)))
        pl.when(rights & no_left)(lambda: whole_chunk(slice(QT, QP)))
        done = (lefts & rights) | (lefts & no_right) | (rights & no_left)

        @pl.when(jnp.logical_not(done))
        def _():
            for half in range(2):
                left, right = need[half]

                def take(lanes):
                    rows = pl.ds(pl.multiple_of(j * KT + half * KC, KC), KC)
                    values = val_ref[j, :, half * KC : (half + 1) * KC]
                    absorb(key_ref[rows, :], values, t, lanes)

                pl.when(left & right)(lambda: take(slice(0, QP)))
                pl.when(left & jnp.logical_not(right))(lambda: take(slice(0, QT)))
                pl.when(right & jnp.logical_not(left))(lambda: take(slice(QT, QP)))

        return carry

    lax.fori_loop(0, NY * 2, visit, 0)

    row8 = lax.broadcasted_iota(jnp.int32, (8, QT), 0)
    lane_m = lax.broadcasted_iota(jnp.int32, (KEPT, 128), 1)
    for t in range(NY):
        pair, lanes = t // 2, slice(t % 2 * QT, t % 2 * QT + QT)
        sums = acc_ref[pair, HD : HD + 1, lanes]
        stats = jnp.zeros((8, QT), F32)
        for number, piece in enumerate(pieces(top_ref[pair, :1, lanes]) + pieces(sums)):
            stats = jnp.where(row8 == number, piece, stats)
        whole = jnp.concatenate(
            [acc_ref[pair, :HD, lanes] * (1.0 / jnp.where(sums > 0.0, sums, 1.0)), stats], axis=0
        )
        for c in range(NB):
            skip = c * TOK // 128 * 128
            moved = whole[:, skip : min(skip + 256, QT)]
            if c:
                moved = pltpu.roll(moved, moved.shape[1] - (c * TOK - skip), 1)
            moved = moved[:, :128]
            rest = moved[KEPT:HD]
            thirds = [pltpu.roll(rest, (TOK - 32 * k) % 128, 1) for k in range(3)]
            kept = jnp.where(lane_m < TOK, moved[:KEPT], jnp.concatenate(thirds, axis=0))
            out_ref[t * NB + c] = jnp.concatenate([kept, moved[HD:]], axis=0).astype(BF)


def merge_kernel(part_ref, w_ref, out_ref, att_ref):
    lane_r = lax.broadcasted_iota(jnp.int32, (HD - KEPT, 128), 1)
    stat = part_ref[:, KEPT:, :].astype(F32)
    tops = stat[:, 0] + stat[:, 1] + stat[:, 2]
    sums = stat[:, 3] + stat[:, 4] + stat[:, 5]
    for h in range(6):
        own = [d for d in range(NG) if HEAD_OF[d] == h]
        rows = slice(own[0], own[-1] + 1)
        top = jnp.max(tops[rows], axis=0, keepdims=True)
        scaled = jnp.exp(tops[rows] - top) * sums[rows]
        total = jnp.sum(scaled, axis=0, keepdims=True)
        shares = scaled / jnp.where(total > 0.0, total, 1.0)
        mixed = jnp.zeros((HD, 128), F32)
        for i, d in enumerate(own):
            part = part_ref[d, :KEPT, :].astype(F32)
            thirds = [
                pltpu.roll(part[16 * k : 16 * k + 16], (32 * k + 128 - TOK) % 128, 1)
                for k in range(3)
            ]
            rest = jnp.where(
                lane_r < 32, thirds[0], jnp.where(lane_r < 64, thirds[1], thirds[2])
            )
            mixed += shares[i : i + 1] * jnp.concatenate([part, rest], axis=0)
        att_ref[HD * h : HD * h + HD, :] = mixed
    attended = att_ref[...].T[:TOK].astype(BF)
    for j in range(NHEAD):
        out_ref[j] = jnp.dot(
            attended, w_ref[:, 384 * j : 384 * j + 384], preferred_element_type=F32
        ).astype(BF)


def split2(x):
    hi = x.astype(BF)
    return hi, (x - hi.astype(F32)).astype(BF)


def stream_kernel(
    scal_ref, term_ref, hid_ref, gate_ref, shift_ref, scale_ref, w_ref, hid_out, msg_ref
):
    first_len, base = scal_ref[0], scal_ref[3]
    projected = term_ref[0].astype(F32)
    for j in range(1, NHEAD):
        projected += term_ref[j].astype(F32)
    pos = base + lax.broadcasted_iota(jnp.int32, (TOK, 384), 0)
    first, second = pos < first_len, pos < LEN_ALL

    def per_row(table):
        return jnp.where(first, table[0:1], jnp.where(second, table[1:2], 0.0))

    gate, shift = gate_ref[...].astype(F32), shift_ref[...].astype(F32)
    factor = 1.0 + scale_ref[...].astype(F32)
    x = (hid_ref[...].astype(F32) + per_row(gate) * projected).astype(BF)
    hid_out[...] = x
    xf = x.astype(F32)
    own_mean = jnp.sum(xf, axis=1, keepdims=True) * (1.0 / 384)
    scaled = jnp.concatenate(
        [(xf - own_mean) * per_row(factor), factor, shift, jnp.zeros((28, 384), F32)], axis=0
    )
    sq_hi, sq_lo = split2(xf * xf)
    ones = jnp.ones((8, 384), BF)

    def turn(left, right):
        return lax.dot_general(left, right, (((1,), (1,)), ((), ())), preferred_element_type=F32)

    high, rest = split2(scaled)
    w = w_ref[...]
    a = turn(w, high) + turn(w, rest)
    left = pltpu.roll(a - a.astype(BF).astype(F32), 4, 1)
    lane = lax.broadcasted_iota(jnp.int32, (64, 128), 1)
    a = jnp.where((lane >= TOK + 4) & (lane < TOK + 8), left, a).astype(BF)
    total = turn(ones, x)
    squares = turn(ones, sq_hi) + turn(ones, sq_lo)
    rows8 = lax.broadcasted_iota(jnp.int32, (8, TOK), 0)
    tail = jnp.zeros((8, TOK), F32)
    for number, piece in enumerate(pieces(total) + pieces(squares)):
        tail = jnp.where(rows8 == number, piece, tail)
    tail = jnp.concatenate([tail, jnp.zeros((8, 128 - TOK), F32)], axis=1)
    message = jnp.concatenate([a.astype(F32), tail], axis=0).astype(BF)
    for j in range(NHEAD):
        msg_ref[j] = message


def step_kernel(scal_ref, coef_ref, msg_ref, lat_ref, clean_ref, prev_ref):
    first_len, base = scal_ref[0], scal_ref[3]
    pos = base + lax.broadcasted_iota(jnp.int32, (64, TOK), 1)
    first, live = pos < first_len, pos < LEN_ALL
    parts = [msg_ref[j].astype(F32) for j in range(NHEAD)]
    sums = [p[64:65, :TOK] + p[65:66, :TOK] + p[66:67, :TOK] for p in parts]
    squares = [p[67:68, :TOK] + p[68:69, :TOK] + p[69:70, :TOK] for p in parts]
    mean, square = sums[0], squares[0]
    for j in range(1, NHEAD):
        mean, square = mean + sums[j], square + squares[j]
    mean, square = mean * (1.0 / D), square * (1.0 / D)
    var = square - mean * mean
    scaled, shifted = jnp.zeros((64, TOK), F32), jnp.zeros((64, 128), F32)
    for p, own in zip(parts, sums):
        scale_w = jnp.where(
            first,
            p[:64, TOK : TOK + 1] + p[:64, TOK + 4 : TOK + 5],
            p[:64, TOK + 1 : TOK + 2] + p[:64, TOK + 5 : TOK + 6],
        )
        scaled += p[:64, :TOK] + (own * (1.0 / 384) - mean) * scale_w
        shifted += p[:64]
    shift_w = jnp.where(
        first,
        shifted[:, TOK + 2 : TOK + 3] + shifted[:, TOK + 6 : TOK + 7],
        shifted[:, TOK + 3 : TOK + 4] + shifted[:, TOK + 7 : TOK + 8],
    )
    velocity = lax.rsqrt(var + EPSILON) * scaled + shift_w
    latent = lat_ref[...]

    def row_coef(i):
        return jnp.where(first, coef_ref[2 * i], coef_ref[2 * i + 1])

    root_a, root_1a, root_q, root_1q = (row_coef(i) for i in range(4))
    clean = root_a * latent - root_1a * velocity
    noise = root_1a * latent + root_a * velocity
    stepped = root_q * clean + root_1q * noise
    clean_ref[...] = jnp.where(live, clean, 0.0)
    prev_ref[...] = jnp.where(live, stepped, 0.0)


def alpha_table():
    betas = np.linspace(0.00085**0.5, 0.012**0.5, TRAIN_STEPS) ** 2
    return np.cumprod(1.0 - betas).astype(np.float32)


TOKEN_AXES = ("y", "a", "c", "core")
NEAR_Z = 1


def core_groups():
    def index(y, a, c, core):
        return ((y * NA + a) * NB + c) * NC + core

    near, far = [], []
    for core in range(NC):
        if core == NEAR_Z:
            near += [[index(y, a, c, core) for a in range(NA) for c in range(NB)] for y in range(NY)]
            far += [[index(y, a, c, core) for y in range(NY)] for a in range(NA) for c in range(NB)]
        else:
            near += [[index(y, a, c, core) for y in range(NY) for c in range(NB)] for a in range(NA)]
            far += [[index(y, a, c, core) for a in range(NA)] for y in range(NY) for c in range(NB)]
    return near, far


def request_of(position, first_len):
    return jnp.where(
        position < 0, -1, jnp.where(position < first_len, 0, jnp.where(position < LEN_ALL, 1, 2))
    )


def shards(
    lengths,
    step_index,
    query_act,
    key_act,
    value_act,
    hidden,
    attn_weight,
    gate_mod,
    shift_mod,
    scale_mod,
    proj_weight,
    latent,
):
    y, a, c = lax.axis_index("y"), lax.axis_index("a"), lax.axis_index("c")
    near_z = lax.axis_index("core") == NEAR_Z
    seq = (y * NA + a) * NB + c
    member = jnp.where(near_z, a, y) * NB + c
    first_len = lengths[0]
    size = jnp.where(member < 12, 32, 48)
    part = jnp.where(member < 12, member % 3, member % 2)
    row_tok, tile_tok = NA * NB * TOK, NB * TOK
    scal = jnp.stack(
        [
            first_len,
            size,
            part * size,
            seq * TOK,
            jnp.where(near_z, y * row_tok, a * tile_tok),
            jnp.where(near_z, tile_tok, row_tok),
            jnp.where(near_z, NA, 1),
            jnp.where(near_z, 1, NA),
        ]
    ).astype(jnp.int32)
    near, far = core_groups()
    in_smem = pl.BlockSpec(memory_space=SMEM)
    big = pltpu.CompilerParams(vmem_limit_bytes=24 * 1024 * 1024)
    small = pltpu.CompilerParams(vmem_limit_bytes=8 * 1024 * 1024)

    any_vmem = pl.BlockSpec(memory_space=VMEM)

    table = jnp.asarray(alpha_table())
    alpha_now = table[step_index]
    alpha_prev = table[step_index - STEP_GAP]
    coef = jnp.concatenate(
        [
            jnp.sqrt(alpha_now),
            jnp.sqrt(1.0 - alpha_now),
            jnp.sqrt(alpha_prev),
            jnp.sqrt(1.0 - alpha_prev),
        ]
    )
    packed = pl.pallas_call(
        pack_kernel, out_shape=jax.ShapeDtypeStruct((NG, TOK, 128), BF), name="pack"
    )(query_act, key_act, value_act)
    mine = lax.all_to_all(packed, TOKEN_AXES, 0, 0, tiled=True, axis_index_groups=near)
    mine, coef = lax.optimization_barrier((mine, coef))
    keyvals = lax.all_gather(
        mine[:, HALF:].reshape(NG * HALF, 128),
        TOKEN_AXES,
        axis=0,
        tiled=True,
        axis_index_groups=far,
    )
    partial = pl.pallas_call(
        attend_kernel,
        out_shape=jax.ShapeDtypeStruct((NG, KEPT + 8, 128), BF),
        in_specs=[in_smem, any_vmem, any_vmem],
        out_specs=any_vmem,
        scratch_shapes=[
            VMEM((NY * KT, 256), BF),
            VMEM((NY, ROWS, KT), BF),
            VMEM((2, 256, QP), BF),
            VMEM((2, 8, QP), F32),
            VMEM((2, ROWS, QP), F32),
        ],
        compiler_params=big,
        name="attend",
    )(scal, mine, keyvals)
    parts = lax.all_to_all(partial, TOKEN_AXES, 0, 0, tiled=True, axis_index_groups=near)
    term = pl.pallas_call(
        merge_kernel,
        out_shape=jax.ShapeDtypeStruct((NHEAD, TOK, 384), BF),
        in_specs=[any_vmem, any_vmem],
        out_specs=any_vmem,
        scratch_shapes=[VMEM((384, 128), F32)],
        compiler_params=big,
        name="merge",
    )(parts, attn_weight)
    terms = lax.all_to_all(term, ("x", "core"), 0, 0, tiled=True)
    hidden_out, message = pl.pallas_call(
        stream_kernel,
        out_shape=(
            jax.ShapeDtypeStruct((TOK, 384), BF),
            jax.ShapeDtypeStruct((NHEAD, 72, 128), BF),
        ),
        in_specs=[in_smem] + [any_vmem] * 6,
        compiler_params=small,
        name="stream",
    )(scal, terms, hidden, gate_mod, shift_mod, scale_mod, proj_weight.T)
    message = lax.all_to_all(message, ("x", "core"), 0, 0, tiled=True)
    clean, stepped = pl.pallas_call(
        step_kernel,
        out_shape=(jax.ShapeDtypeStruct((64, TOK), F32),) * 2,
        in_specs=[in_smem, in_smem, any_vmem, any_vmem],
        compiler_params=small,
        name="ddim",
    )(scal, coef, message, latent.T)
    pairs = []
    for s in range(NY * NA * NB):
        for x in range(NX):
            up, down = (s * NX + x) * NC, (s * NX + x) * NC + 1
            if s + 1 < NY * NA * NB:
                pairs.append((up, up + NX * NC))
            if s > 0:
                pairs.append((down, down - NX * NC))
    got = lax.ppermute(stepped, ("y", "a", "c", "x", "core"), pairs)
    both = lax.all_gather(got, "core")
    offsets = jnp.arange(RIM, dtype=jnp.int32)
    start = seq * TOK
    lower_ok = request_of(start - RIM + offsets, first_len) == request_of(start, first_len)
    upper_ok = request_of(start + TOK + offsets, first_len) == request_of(
        start + TOK - 1, first_len
    )
    lower_ok &= start > 0
    upper_ok &= start + TOK < NY * NA * NB * TOK
    rims = jnp.concatenate(
        [
            jnp.where(lower_ok[None], both[0, :, TOK - RIM :], 0.0),
            jnp.where(upper_ok[None], both[1, :, :RIM], 0.0),
        ],
        axis=1,
    )
    return hidden_out, clean.T, stepped.T, rims.T


def solution(mesh):
    grid = Mesh(mesh.devices.reshape(NY, NA, NB, NX, NC), ("y", "a", "c", "x", "core"))
    seq, head = ("y", "a", "c"), ("x", "core")
    in_specs = (
        P(),
        P(),
        P(seq, head),
        P(seq, head),
        P(seq, head),
        P(seq, head),
        P(head, None),
        P(None, head),
        P(None, head),
        P(None, head),
        P(head, None),
        P(seq, None),
    )
    out_specs = (P(seq, head), P(seq, None), P(seq, None), P(seq, None))
    return jax.shard_map(shards, mesh=grid, in_specs=in_specs, out_specs=out_specs, check_vma=False)
```
